256 devices in a mesh: seq: 64 (over y, z, core), head: 4 (over x).
Axes of the slice: x: 4, y: 4, z: 8, core: 2. Of those that a mesh axis runs over, the one named last changes fastest.
Arguments:
- queries: bfloat16 [65536, 1024], P('seq', 'head'), may hold values from -6 to 6
- keys: bfloat16 [65536, 1024], P('seq', 'head'), may hold values from -12 to 12
- values: bfloat16 [65536, 1024], P('seq', 'head'), may hold values from -6 to 6
- out_weight: bfloat16 [1024, 1024], P('head'), may hold values from -0.1875 to 0.1875
- cotangent: bfloat16 [65536, 1024], P('seq', 'head'), may hold values from -6 to 6
Outputs:
- output: bfloat16 [65536, 1024], P('seq', 'head')
- query_grad: bfloat16 [65536, 1024], P('seq', 'head')
- key_grad: bfloat16 [65536, 1024], P('seq', 'head')
- value_grad: bfloat16 [65536, 1024], P('seq', 'head')
- weight_grad: float32 [1024, 1024], P('head')
The draws below stay inside these ranges and needn't reach their ends.
All inputs are finite; a program needn't handle non-finite values.
Results may differ from the reference program's by a relative error of at most 0.015.
Values may be sent and summed in bfloat16 or wider, within the bound.
A program may use at most 128 MiB of HBM per device.

```python
import jax
import jax.numpy as jnp
from jax import lax

BLOCK = 1024
TILE = 128
DH = 128
HEADS = 8
D = 1024
TOKENS = 65536
N_SEQ = 64


def draw_queries(key, part):
    base = jnp.clip(jax.random.normal(jax.random.fold_in(key, 1), (TOKENS, D), jnp.float32), -6.0, 6.0)
    return base.astype(jnp.bfloat16)


def draw_keys(key, part):
    base = jnp.clip(2.5 * jax.random.normal(jax.random.fold_in(key, 2), (TOKENS, D), jnp.float32), -12.0, 12.0)
    return base.astype(jnp.bfloat16)


def steps_of(stream_key, extent, shards, smallest, top_value):
    loudness, own = 1.0, jax.random.fold_in(stream_key, 6)
    for position, blocks in shards:
        heights = jnp.exp(jax.random.uniform(jax.random.fold_in(own, position), (blocks,), jnp.float32, smallest / len(shards), top_value / len(shards)))
        loudness = loudness * jnp.repeat(heights, extent[position] // blocks).reshape([-1 if axis == position else 1 for axis in range(len(extent))])
    return loudness


def bell_draw(key, shape, deviation, limit, shards=(), kind=jnp.bfloat16):
    entries = deviation * jax.random.normal(key, shape, jnp.float32)
    if shards:
        entries = entries * steps_of(key, shape, shards, -0.22, 0.18)
    return jnp.clip(entries, -limit, limit).astype(kind)


def setup_inputs(seed: int = 0) -> dict:
    splits = jax.random.split(jax.random.key(seed), 6)
    return {
        "queries": draw_queries(jax.random.fold_in(splits[5], 71), 0),
        "keys": draw_keys(jax.random.fold_in(splits[5], 71), 0),
        "values": bell_draw(splits[2], (TOKENS, D), 1.0, 6.0, ((0, 64), (1, 4))),
        "out_weight": bell_draw(splits[3], (D, D), D ** -0.5, 0.1875, ((0, 4),)),
        "cotangent": bell_draw(splits[4], (TOKENS, D), 1.0, 6.0, ((0, 64), (1, 4))),
    }


def attend(query_blk, all_keys, all_values, allowed, dattn_blk):
    scale = DH ** -0.5
    scores = jnp.einsum('qhd,khd->hqk', query_blk.astype(jnp.float32), all_keys.astype(jnp.float32)) * scale
    scores = jnp.where(allowed[None], scores, -jnp.inf)
    top = jnp.max(scores, axis=-1, keepdims=True)
    expo = jnp.exp(scores - top)
    prob = expo / jnp.sum(expo, axis=-1, keepdims=True)
    prob_low = lax.optimization_barrier(prob.astype(jnp.bfloat16))
    attn = jnp.einsum('hqk,khd->qhd', prob_low.astype(jnp.float32), all_values.astype(jnp.float32)).astype(jnp.bfloat16)
    dattn32 = dattn_blk.astype(jnp.float32)
    dprob = jnp.einsum('qhd,khd->hqk', dattn32, all_values.astype(jnp.float32))
    value_terms = jnp.einsum('hqk,qhd->khd', prob_low.astype(jnp.float32), dattn32)
    delta = jnp.sum(prob * dprob, axis=-1, keepdims=True)
    dscore = lax.optimization_barrier((prob * (dprob - delta)).astype(jnp.bfloat16))
    query_terms = jnp.einsum('hqk,khd->qhd', dscore.astype(jnp.float32), all_keys.astype(jnp.float32)) * scale
    key_terms = jnp.einsum('hqk,qhd->khd', dscore.astype(jnp.float32), query_blk.astype(jnp.float32)) * scale
    return attn, query_terms, key_terms, value_terms


def reference(queries, keys, values, out_weight, cotangent):
    count = N_SEQ
    levels = count.bit_length() - 1
    dattn = lax.optimization_barrier(jnp.dot(cotangent, out_weight.T, preferred_element_type=jnp.float32).astype(jnp.bfloat16))
    query4 = queries.reshape(count, BLOCK, HEADS, DH)
    key4 = keys.reshape(count, BLOCK, HEADS, DH)
    value4 = values.reshape(count, BLOCK, HEADS, DH)
    dattn4 = dattn.reshape(count, BLOCK, HEADS, DH)
    key_tiles = key4[:, BLOCK - TILE:]
    value_tiles = value4[:, BLOCK - TILE:]
    offsets = (2 ** jnp.arange(levels)).astype(jnp.int32)
    causal = jnp.arange(BLOCK)[:, None] >= jnp.arange(BLOCK)[None, :]

    def one_block(block_id):
        source = block_id - offsets
        valid = source >= 0
        clipped = jnp.maximum(source, 0).astype(jnp.int32)
        far_keys = key_tiles[clipped].reshape(levels * TILE, HEADS, DH)
        far_values = value_tiles[clipped].reshape(levels * TILE, HEADS, DH)
        tile_ok = jnp.broadcast_to(jnp.repeat(valid, TILE)[None, :], (BLOCK, levels * TILE))
        allowed = jnp.concatenate([causal, tile_ok], axis=1)
        all_keys = jnp.concatenate([key4[block_id], far_keys], axis=0)
        all_values = jnp.concatenate([value4[block_id], far_values], axis=0)
        attn, query_terms, key_terms, value_terms = attend(query4[block_id], all_keys, all_values, allowed, dattn4[block_id])
        return attn, query_terms, key_terms[:BLOCK], value_terms[:BLOCK], key_terms[BLOCK:], value_terms[BLOCK:]

    attn, query_terms, key_own, value_own, key_far, value_far = lax.map(one_block, jnp.arange(count, dtype=jnp.int32))
    key_far = key_far.reshape(count, levels, TILE, HEADS, DH)
    value_far = value_far.reshape(count, levels, TILE, HEADS, DH)
    key_tail = key_own[:, BLOCK - TILE:]
    value_tail = value_own[:, BLOCK - TILE:]
    for level_idx in range(levels):
        reach = 2 ** level_idx
        key_tail = key_tail.at[:count - reach].add(key_far[reach:, level_idx])
        value_tail = value_tail.at[:count - reach].add(value_far[reach:, level_idx])
    key_own = jnp.concatenate([key_own[:, :BLOCK - TILE], key_tail], axis=1)
    value_own = jnp.concatenate([value_own[:, :BLOCK - TILE], value_tail], axis=1)
    attn = attn.reshape(TOKENS, D)
    output = jnp.dot(attn, out_weight, preferred_element_type=jnp.float32).astype(jnp.bfloat16)
    weight_grad = jnp.dot(attn.T, cotangent, preferred_element_type=jnp.float32)
    query_grad = query_terms.reshape(TOKENS, D).astype(jnp.bfloat16)
    key_grad = key_own.reshape(TOKENS, D).astype(jnp.bfloat16)
    value_grad = value_own.reshape(TOKENS, D).astype(jnp.bfloat16)
    return (output, query_grad, key_grad, value_grad, weight_grad)
```

```python
import functools

import jax
import jax.numpy as jnp
import numpy as np
from jax import lax
from jax.experimental import pallas as pl
from jax.experimental.pallas import tpu as pltpu
from jax.sharding import PartitionSpec as P

TILE = 128
DH = 128
STEP = 256
MESH = pl.DeviceIdType.MESH
F32 = jnp.float32
BF16 = jnp.bfloat16
NEG = -1e30
FAR = 3e38


def mm(a, b):
    return jnp.dot(a, b, preferred_element_type=F32)


def mm_t(a, b):
    return lax.dot_general(a, b, (((1,), (1,)), ((), ())), preferred_element_type=F32)


def kernel(
    plan,
    q_ref, k_ref, v_ref, w_ref, c_ref,
    out_ref, dq_ref, dk_ref, dv_ref, wg_ref,
    ktile, vtile, kback, vback, ksend, vsend,
    cot, kt, vt, ktt, vtt,
    s_own, s_tile, e_own, e_tile, d_own, d_tile,
    acc, attn_t32, attn_t, attn, m_o, l_o, m_t, r_o, r_t, del_o, del_t,
    datt_t, datt_o, datt_s, datt_on, datt_sn, dqt,
    p_send, p_own, p_from,
    g_send, g_from, g_part, g_ysend, g_yfrom, g_y, g_zsend, g_zfrom, g_full,
    fwd_s, fwd_r, bwd_s, bwd_r, x_s, x_r, w_s, w_r,
):
    seq, heads_x, levels, ny, nz, ystride = plan
    rows, width = q_ref.shape
    nh = width // DH
    nb = rows // STEP
    tail = rows - TILE
    b = lax.axis_index("seq")
    x = lax.axis_index("head")
    core = lax.rem(b, 2)
    yy = b // ystride
    zz = lax.rem(b, ystride) // 2
    right = lax.rem(x + 1, heads_x)
    left = lax.rem(x + heads_x - 1, heads_x)
    over = lax.rem(x + 2, heads_x)
    factor = float(DH ** (-0.5) * np.log2(np.e))
    scale = DH ** (-0.5)

    def ahead(l):
        return (lax.rem(b + 2**l, seq), x)

    def behind(l):
        return (lax.rem(b + seq - 2**l, seq), x)

    sibling = (b + 1 - 2 * core, x)

    def ypeer(d):
        return lax.rem(yy + d, ny)

    def zpeer(d):
        return lax.rem(zz + d, nz)

    def yid(d):
        return (ypeer(d) * ystride + zz * 2 + core, x)

    def zid(d):
        return (yy * ystride + zpeer(d) * 2 + core, x)

    peers = [ahead(l) for l in range(levels)] + [behind(l) for l in range(levels)]
    peers += [sibling] + [yid(d) for d in range(1, ny)] + [zid(d) for d in range(1, nz)]
    peers += [(b, right), (b, left), (b, over)]
    barrier = pltpu.get_barrier_semaphore()
    for peer in peers:
        pl.semaphore_signal(barrier, inc=1, device_id=peer, device_id_type=MESH)

    def remote(src, dst, sems, semr, idx, to):
        c = pltpu.make_async_remote_copy(
            src_ref=src, dst_ref=dst, send_sem=sems.at[idx], recv_sem=semr.at[idx],
            device_id=to, device_id_type=MESH,
        )
        c.start()
        return c

    def hs(h):
        return pl.ds(pl.multiple_of(h * DH, DH), DH)

    kt[...] = k_ref[...].T
    vt[...] = v_ref[...].T
    pl.semaphore_wait(barrier, len(peers))

    sent = []
    order = list(range(levels))[::-1]
    ktc, vtc = {}, {}
    for l in order:
        span = pl.ds(l * TILE, TILE)
        ktc[l] = remote(k_ref.at[pl.ds(tail, TILE)], ktile.at[span], fwd_s, fwd_r, 2 * l, ahead(l))
        vtc[l] = remote(v_ref.at[pl.ds(tail, TILE)], vtile.at[span], fwd_s, fwd_r, 2 * l + 1, ahead(l))
        sent += [ktc[l], vtc[l]]

    half = rows // 2
    lo, hi = pl.ds(0, half), pl.ds(half, half)
    mine = cot.at[x]
    to_right_lo = remote(c_ref.at[lo], mine.at[lo], x_s, x_r, 0, (b, right))
    to_left_hi = remote(c_ref.at[hi], mine.at[hi], x_s, x_r, 1, (b, left))
    to_right_hi = remote(c_ref.at[hi], mine.at[hi], x_s, x_r, 2, (b, right))
    to_left_lo = remote(c_ref.at[lo], mine.at[lo], x_s, x_r, 3, (b, left))
    sent += [to_right_lo, to_left_hi, to_right_hi, to_left_lo]

    def own_fwd(h, _):
        for i in range(nb):
            cols = pl.ds(i * STEP, STEP)
            qi = q_ref[cols, hs(h)]
            top = jnp.full((1, STEP), NEG, F32)
            for j in range(i + 1):
                s = mm_t(k_ref[pl.ds(j * STEP, STEP), hs(h)], qi)
                if j == i:
                    key = lax.broadcasted_iota(jnp.int32, (STEP, STEP), 0)
                    query = lax.broadcasted_iota(jnp.int32, (STEP, STEP), 1)
                    s = jnp.where(key <= query, s, NEG)
                s_own[pl.ds(j * STEP, STEP), :] = s
                top = jnp.maximum(top, jnp.max(s, axis=0, keepdims=True))
            m_o[h, :, cols] = top
            total = jnp.zeros((1, STEP), F32)
            part = jnp.zeros((DH, STEP), F32)
            for j in range(i + 1):
                e = jnp.exp2((s_own[pl.ds(j * STEP, STEP), :] - top) * factor)
                total = total + jnp.sum(e, axis=0, keepdims=True)
                e = e.astype(BF16)
                e_own[h, pl.ds(j * STEP, STEP), cols] = e
                part = part + mm(vt[hs(h), pl.ds(j * STEP, STEP)], e)
            l_o[h, :, cols] = total
            acc[hs(h), cols] = part
        return 0

    lax.fori_loop(0, nh, own_fwd, 0)

    cot[x] = c_ref[...]
    to_right_lo.wait_recv()
    pass_lo = remote(cot.at[left, lo], cot.at[left, lo], x_s, x_r, 4, (b, right))
    to_left_hi.wait_recv()
    pass_hi = remote(cot.at[right, hi], cot.at[right, hi], x_s, x_r, 5, (b, left))
    sent += [pass_lo, pass_hi]

    for h in range(nh):
        m_t[h] = jnp.full((1, rows), NEG, F32)
    valid = {l: b >= 2**l for l in range(levels)}
    for l in order:
        span = pl.ds(l * TILE, TILE)
        ktc[l].wait_recv()
        vtc[l].wait_recv()

        def tile_scores(h, _):
            for i in range(nb):
                cols = pl.ds(i * STEP, STEP)
                s = mm_t(ktile[span, hs(h)], q_ref[cols, hs(h)])
                s_tile[h, span, cols] = s
                top = jnp.max(s, axis=0, keepdims=True)
                m_t[h, :, cols] = jnp.maximum(m_t[h, :, cols], jnp.where(valid[l], top, NEG))
            return 0

        lax.fori_loop(0, nh, tile_scores, 0)
        ktt[:, span] = ktile[span, :].T
        vtt[:, span] = vtile[span, :].T

    def tile_fwd(h, _):
        for i in range(nb):
            cols = pl.ds(i * STEP, STEP)
            top = m_t[h, :, cols]
            total = jnp.zeros((1, STEP), F32)
            part = jnp.zeros((DH, STEP), F32)
            for l in range(levels):
                span = pl.ds(l * TILE, TILE)
                shift = jnp.where(valid[l], top, FAR)
                e = jnp.exp2((s_tile[h, span, cols] - shift) * factor)
                total = total + jnp.sum(e, axis=0, keepdims=True)
                e_tile[h, span, cols] = e.astype(BF16)
            part = mm(vtt[hs(h), :], e_tile[h, :, cols])
            mo = m_o[h, :, cols]
            m = jnp.maximum(mo, top)
            fo = jnp.exp2((mo - m) * factor)
            ft = jnp.exp2((top - m) * factor)
            inv = 1.0 / (fo * l_o[h, :, cols] + ft * total)
            fo = fo * inv
            ft = ft * inv
            r_o[h, :, cols] = fo
            r_t[h, :, cols] = ft
            at = acc[hs(h), cols] * fo + part * ft
            attn_t32[hs(h), cols] = at
            attn_t[hs(h), cols] = at.astype(BF16)
            attn[cols, hs(h)] = at.T.astype(BF16)
        return 0

    lax.fori_loop(0, nh, tile_fwd, 0)

    def wcols(at):
        return pl.ds(pl.multiple_of(at * width, width), width)

    p_send[0] = mm(attn[...], w_ref[:, wcols(over)]).astype(BF16)
    o_lo = remote(p_send.at[0, lo], p_from.at[0, lo], x_s, x_r, 6, (b, right))
    o_hi = remote(p_send.at[0, hi], p_from.at[1, hi], x_s, x_r, 7, (b, left))
    p_send[1] = mm(attn[...], w_ref[:, wcols(right)]).astype(BF16)
    r_hi = remote(p_send.at[1, hi], p_from.at[2, hi], x_s, x_r, 8, (b, right))
    p_send[2] = mm(attn[...], w_ref[:, wcols(left)]).astype(BF16)
    l_lo = remote(p_send.at[2, lo], p_from.at[3, lo], x_s, x_r, 9, (b, left))
    sent += [o_lo, o_hi, r_hi, l_lo]
    p_own[...] = mm(attn[...], w_ref[:, wcols(x)])

    to_right_hi.wait_recv()
    to_left_lo.wait_recv()
    pass_lo.wait_recv()
    pass_hi.wait_recv()

    for i in range(nb):
        cols = pl.ds(i * STEP, STEP)
        g = jnp.zeros((width, STEP), F32)
        for j in range(heads_x):
            g = g + mm_t(w_ref[:, pl.ds(j * width, width)], cot[j, cols, :])
        datt_t[:, cols] = g.astype(BF16)

    def spread(h, _):
        for i in range(nb):
            cols = pl.ds(i * STEP, STEP)
            g = datt_t[hs(h), cols].astype(F32)
            at = attn_t32[hs(h), cols]
            go = (g * r_o[h, :, cols]).astype(BF16)
            gt = (g * r_t[h, :, cols]).astype(BF16)
            datt_o[hs(h), cols] = go
            datt_s[hs(h), cols] = gt
            go = go.astype(F32)
            gt = gt.astype(F32)
            del_o[h, :, cols] = jnp.sum(go * at, axis=0, keepdims=True)
            del_t[h, :, cols] = jnp.sum(gt * at, axis=0, keepdims=True)
            datt_on[cols, hs(h)] = go.T.astype(BF16)
            datt_sn[cols, hs(h)] = gt.T.astype(BF16)
        return 0

    lax.fori_loop(0, nh, spread, 0)

    gh = width // 2
    for j in range(heads_x):
        g_send[:, pl.ds(j * width, width)] = mm(
            attn_t[pl.ds(pl.multiple_of((1 - core) * gh, gh), gh), :], cot[j]
        ).astype(BF16)
    g_core = remote(g_send, g_from, w_s, w_r, 0, sibling)
    sent.append(g_core)
    for j in range(heads_x):
        g_part[:, pl.ds(j * width, width)] = mm(
            attn_t[pl.ds(pl.multiple_of(core * gh, gh), gh), :], cot[j]
        )

    kbc, vbc = {}, {}

    def tile_bwd_for(l):
        span = pl.ds(l * TILE, TILE)

        def tile_bwd(h, _):
            for i in range(nb):
                cols = pl.ds(i * STEP, STEP)
                dp = mm(vtile[span, hs(h)], datt_s[hs(h), cols])
                d = e_tile[h, span, cols].astype(F32) * (dp - del_t[h, :, cols])
                d_tile[h, span, cols] = d.astype(BF16)
            ksend[span, hs(h)] = (mm(d_tile[h, span, :], q_ref[:, hs(h)]) * scale).astype(BF16)
            vsend[span, hs(h)] = mm(e_tile[h, span, :], datt_sn[:, hs(h)]).astype(BF16)
            return 0

        lax.fori_loop(0, nh, tile_bwd, 0)
        kbc[l] = remote(ksend.at[span], kback.at[span], bwd_s, bwd_r, 2 * l, behind(l))
        vbc[l] = remote(vsend.at[span], vback.at[span], bwd_s, bwd_r, 2 * l + 1, behind(l))

    for l in order[: levels // 2]:
        tile_bwd_for(l)

    gy = gh // ny
    g_core.wait_recv()
    g_part[...] = g_part[...] + g_from[...].astype(F32)
    g_ysend[...] = g_part[...].astype(BF16)

    def yrows(at):
        return pl.ds(pl.multiple_of(at * gy, gy), gy)

    ysum = [
        remote(g_ysend.at[yrows(ypeer(d))], g_yfrom.at[d], w_s, w_r, d, yid(d)) for d in range(1, ny)
    ]
    sent += ysum

    for l in order[levels // 2 :]:
        tile_bwd_for(l)
    for l in order:
        sent += [kbc[l], vbc[l]]

    o_lo.wait_recv()
    p_send[1, lo, :] = (p_send[1, lo, :].astype(F32) + p_from[0, lo, :].astype(F32)).astype(BF16)
    pass_r = remote(p_send.at[1, lo], p_from.at[2, lo], x_s, x_r, 10, (b, right))
    o_hi.wait_recv()
    p_send[2, hi, :] = (p_send[2, hi, :].astype(F32) + p_from[1, hi, :].astype(F32)).astype(BF16)
    pass_l = remote(p_send.at[2, hi], p_from.at[3, hi], x_s, x_r, 11, (b, left))
    sent += [pass_r, pass_l]

    gz = heads_x * width // nz

    def zcols(at):
        return pl.ds(pl.multiple_of(at * gz, gz), gz)

    for c in ysum:
        c.wait_recv()
    total = g_part[yrows(yy), :]
    for d in range(1, ny):
        total = total + g_yfrom[d].astype(F32)
    g_y[...] = total
    g_zsend[...] = total.astype(BF16)
    zsum = [
        remote(g_zsend.at[:, zcols(zpeer(d))], g_zfrom.at[d], w_s, w_r, ny + d, zid(d))
        for d in range(1, nz)
    ]
    sent += zsum

    def own_bwd(h, _):
        for j in range(nb):
            span = pl.ds(j * STEP, STEP)
            for i in range(j, nb):
                cols = pl.ds(i * STEP, STEP)
                dp = mm(v_ref[span, hs(h)], datt_o[hs(h), cols])
                d = e_own[h, span, cols].astype(F32) * (dp - del_o[h, :, cols])
                d_own[h, span, cols] = d.astype(BF16)
            rest = pl.ds(j * STEP, rows - j * STEP)
            dk = mm(d_own[h, span, rest], q_ref[rest, hs(h)]) * scale
            dv = mm(e_own[h, span, rest], datt_on[rest, hs(h)])
            dk_ref[span, hs(h)] = dk.astype(BF16)
            dv_ref[span, hs(h)] = dv.astype(BF16)
            if j == nb - 1:
                dqt[0, :, hs(h)] = dk[STEP - TILE :]
                dqt[1, :, hs(h)] = dv[STEP - TILE :]
        for i in range(nb):
            cols = pl.ds(i * STEP, STEP)
            upto = pl.ds(0, (i + 1) * STEP)
            g = mm(kt[hs(h), upto], d_own[h, upto, cols])
            g = g + mm(ktt[hs(h), :], d_tile[h, :, cols])
            dq_ref[cols, hs(h)] = (g * scale).T.astype(BF16)
        return 0

    own_bwd(0, 0)

    for c in zsum:
        c.wait_recv()
    piece = g_y[:, zcols(zz)]
    for d in range(1, nz):
        piece = piece + g_zfrom[d].astype(F32)
    at_rows = pl.ds(pl.multiple_of(core * gh + yy * gy, gy), gy)
    g_full[at_rows, zcols(zz)] = piece.astype(BF16)
    zall = [
        remote(g_full.at[at_rows, zcols(zz)], g_full.at[at_rows, zcols(zz)], w_s, w_r, ny + nz + d, zid(d))
        for d in range(1, nz)
    ]
    sent += zall

    for h in range(1, nh):
        own_bwd(h, 0)

    for c in zall:
        c.wait_recv()
    yall = [
        remote(g_full.at[at_rows], g_full.at[at_rows], w_s, w_r, ny + 2 * nz + d, yid(d))
        for d in range(1, ny)
    ]
    sent += yall

    r_hi.wait_recv()
    l_lo.wait_recv()
    pass_r.wait_recv()
    pass_l.wait_recv()
    out_ref[...] = (p_own[...] + p_from[2].astype(F32) + p_from[3].astype(F32)).astype(BF16)

    for c in yall:
        c.wait_recv()
    core_rows = pl.ds(pl.multiple_of(core * gh, gh), gh)
    g_last = remote(g_full.at[core_rows], g_full.at[core_rows], w_s, w_r, 2 * ny + 2 * nz, sibling)
    sent.append(g_last)

    dk = dqt[0]
    dv = dqt[1]
    for l in order:
        span = pl.ds(l * TILE, TILE)
        kbc[l].wait_recv()
        vbc[l].wait_recv()
        dk = dk + kback[span, :].astype(F32)
        dv = dv + vback[span, :].astype(F32)
    dk_ref[pl.ds(tail, TILE), :] = dk.astype(BF16)
    dv_ref[pl.ds(tail, TILE), :] = dv.astype(BF16)

    g_last.wait_recv()
    wg_ref[...] = g_full[...].astype(F32)
    for c in sent:
        c.wait_send()


def local(plan, queries, keys, values, out_weight, cotangent):
    seq, heads_x, levels, ny, nz, _ = plan
    rows, width = queries.shape
    nh = width // DH
    far = levels * TILE
    wide = heads_x * width
    gh = width // 2
    gy = gh // ny
    gz = wide // nz
    dma = pltpu.SemaphoreType.DMA
    like = [(rows, width)] * 4
    return pl.pallas_call(
        functools.partial(kernel, plan),
        out_shape=[jax.ShapeDtypeStruct(s, BF16) for s in like]
        + [jax.ShapeDtypeStruct((width, wide), F32)],
        in_specs=[pl.BlockSpec(memory_space=pltpu.VMEM)] * 5,
        out_specs=[pl.BlockSpec(memory_space=pltpu.VMEM)] * 5,
        scratch_shapes=[
            pltpu.VMEM((far, width), BF16), pltpu.VMEM((far, width), BF16),
            pltpu.VMEM((far, width), BF16), pltpu.VMEM((far, width), BF16),
            pltpu.VMEM((far, width), BF16), pltpu.VMEM((far, width), BF16),
            pltpu.VMEM((heads_x, rows, width), BF16),
            pltpu.VMEM((width, rows), BF16), pltpu.VMEM((width, rows), BF16),
            pltpu.VMEM((width, far), BF16), pltpu.VMEM((width, far), BF16),
            pltpu.VMEM((rows, STEP), F32), pltpu.VMEM((nh, far, rows), F32),
            pltpu.VMEM((nh, rows, rows), BF16), pltpu.VMEM((nh, far, rows), BF16),
            pltpu.VMEM((nh, rows, rows), BF16), pltpu.VMEM((nh, far, rows), BF16),
            pltpu.VMEM((width, rows), F32), pltpu.VMEM((width, rows), F32),
            pltpu.VMEM((width, rows), BF16), pltpu.VMEM((rows, width), BF16),
        ]
        + [pltpu.VMEM((nh, 1, rows), F32)] * 7
        + [
            pltpu.VMEM((width, rows), BF16), pltpu.VMEM((width, rows), BF16),
            pltpu.VMEM((width, rows), BF16), pltpu.VMEM((rows, width), BF16),
            pltpu.VMEM((rows, width), BF16), pltpu.VMEM((2, TILE, width), F32),
            pltpu.VMEM((3, rows, width), BF16), pltpu.VMEM((rows, width), F32),
            pltpu.VMEM((4, rows, width), BF16),
            pltpu.VMEM((gh, wide), BF16), pltpu.VMEM((gh, wide), BF16),
            pltpu.VMEM((gh, wide), F32), pltpu.VMEM((gh, wide), BF16),
            pltpu.VMEM((ny, gy, wide), BF16), pltpu.VMEM((gy, wide), F32),
            pltpu.VMEM((gy, wide), BF16), pltpu.VMEM((nz, gy, gz), BF16),
            pltpu.VMEM((width, wide), BF16),
            dma((2 * levels,)), dma((2 * levels,)), dma((2 * levels,)), dma((2 * levels,)),
            dma((12,)), dma((12,)),
            dma((2 * ny + 2 * nz + 1,)), dma((2 * ny + 2 * nz + 1,)),
        ],
        compiler_params=pltpu.CompilerParams(
            collective_id=0, has_side_effects=True, vmem_limit_bytes=60 * 1024 * 1024
        ),
        name="layer",
    )(queries, keys, values, out_weight, cotangent)


def solution(mesh):
    seq = mesh.shape["seq"]
    heads_x = mesh.shape["head"]
    levels = seq.bit_length() - 1
    ny = 4 if seq >= 16 else 2
    ystride = seq // ny
    plan = (seq, heads_x, levels, ny, ystride // 2, ystride)
    return jax.shard_map(
        functools.partial(local, plan),
        mesh=mesh,
        in_specs=(
            P("seq", "head"), P("seq", "head"), P("seq", "head"), P("head", None), P("seq", "head"),
        ),
        out_specs=(
            P("seq", "head"), P("seq", "head"), P("seq", "head"), P("seq", "head"), P("head", None),
        ),
        check_vma=False,
    )
```

```python
import functools

import jax
import jax.numpy as jnp
import numpy as np
from jax import lax
from jax.experimental import pallas as pl
from jax.experimental.pallas import tpu as pltpu
from jax.sharding import PartitionSpec as P

TILE = 128
DH = 128
STEP = 256
MESH = pl.DeviceIdType.MESH
F32 = jnp.float32
BF16 = jnp.bfloat16
NEG = -1e30
FAR = 3e38


def mm(a, b):
    return jnp.dot(a, b, preferred_element_type=F32)


def mm_t(a, b):
    return lax.dot_general(a, b, (((1,), (1,)), ((), ())), preferred_element_type=F32)


def kernel(
    plan,
    q_hbm, k_hbm, v_hbm, w_hbm, c_hbm,
    out_ref, dq_ref, dk_ref, dv_ref, wg_ref,
    q_ref, k_ref, v_ref, w_ref,
    ktile, vtile, kback, vback, ksend, vsend, vmid_f, kmid_b, vmid_b, vfar_b, one_b,
    cot, kt, vt, ktt, vtt,
    s_own, s_tile, e_own, e_tile, d_own, d_tile,
    acc, attn_t32, attn_t, attn, m_o, l_o, m_t, r_o, r_t, del_o, del_t,
    datt_t, datt_o, datt_s, datt_on, datt_sn, dqt,
    p_send, p_own, p_from,
    g_send, g_from, g_part, g_ysend, g_yfrom, g_y, g_zsend, g_zfrom, g_full,
    fwd_s, fwd_r, bwd_s, bwd_r, x_s, x_r, w_s, w_r, in_s,
):
    seq, heads_x, levels, ny, nz, ystride = plan
    rows, width = q_hbm.shape
    nh = width // DH
    nb = rows // STEP
    tail = rows - TILE
    b = lax.axis_index("seq")
    x = lax.axis_index("head")
    core = lax.rem(b, 2)
    yy = b // ystride
    zz = lax.rem(b, ystride) // 2
    right = lax.rem(x + 1, heads_x)
    left = lax.rem(x + heads_x - 1, heads_x)
    over = lax.rem(x + 2, heads_x)
    far = levels // 2
    factor = float(DH ** (-0.5) * np.log2(np.e))
    scale = DH ** (-0.5)

    def ahead(l):
        return (lax.rem(b + 2**l, seq), x)

    def behind(l):
        return (lax.rem(b + seq - 2**l, seq), x)

    sibling = (b + 1 - 2 * core, x)

    def ypeer(d):
        return lax.rem(yy + d, ny)

    def zpeer(d):
        return lax.rem(zz + d, nz)

    def yid(d):
        return (ypeer(d) * ystride + zz * 2 + core, x)

    def zid(d):
        return (yy * ystride + zpeer(d) * 2 + core, x)

    def from_z(dz):
        return yy * ystride + lax.rem(zz + dz + nz, nz) * 2 + core

    reach = 2**far
    mid_f = (from_z(-2), x)
    mid_b = (from_z(2), x)
    end_f = (lax.rem(from_z(2) + reach, seq), x)
    end_b = (lax.rem(from_z(-2) - reach + seq, seq), x)
    src_f, src_b = lax.rem(b + seq - reach, seq), lax.rem(b + reach, seq)
    pass_f = (src_f // ystride * ystride + lax.rem(lax.rem(src_f, ystride) // 2 + nz - 2, nz) * 2 + core, x)
    pass_b = (src_b // ystride * ystride + lax.rem(lax.rem(src_b, ystride) // 2 + 2, nz) * 2 + core, x)

    peers = [behind(0), ahead(0), behind(1), ahead(1), behind(far), ahead(far), pass_f, pass_b]
    peers += [yid(d) for d in range(1, ny)] + [zid(d) for d in range(1, nz)]
    peers += [(b, right), (b, left)]
    barrier = pltpu.get_barrier_semaphore()
    for peer in peers:
        pl.semaphore_signal(barrier, inc=1, device_id=peer, device_id_type=MESH)

    def remote(src, dst, sems, semr, idx, to):
        c = pltpu.make_async_remote_copy(
            src_ref=src, dst_ref=dst, send_sem=sems.at[idx], recv_sem=semr.at[idx],
            device_id=to, device_id_type=MESH,
        )
        c.start()
        return c

    def hs(h):
        return pl.ds(pl.multiple_of(h * DH, DH), DH)

    loads = [
        pltpu.make_async_copy(src, dst, in_s.at[n])
        for n, (src, dst) in enumerate(
            [(k_hbm, k_ref), (v_hbm, v_ref), (q_hbm, q_ref), (c_hbm, cot.at[x]), (w_hbm, w_ref)]
        )
    ]
    for c in loads:
        c.start()
    pl.semaphore_wait(barrier, len(peers))

    def rows_of(l):
        return pl.ds(l * TILE, TILE)

    sent = []
    ktc, vtc = {}, {}
    last = pl.ds(tail, TILE)

    def send_k(l):
        ktc[l] = remote(k_hbm.at[last], ktile.at[rows_of(l)], fwd_s, fwd_r, 2 * l, ahead(l))
        sent.append(ktc[l])

    def send_v(l):
        vtc[l] = remote(v_hbm.at[last], vtile.at[rows_of(l)], fwd_s, fwd_r, 2 * l + 1, ahead(l))
        sent.append(vtc[l])

    half = rows // 2
    lo, hi = pl.ds(0, half), pl.ds(half, half)
    mine = cot.at[x]
    send_k(1)
    send_v(1)
    v_mid = remote(v_hbm.at[last], vmid_f, fwd_s, fwd_r, 2 * levels, mid_f)
    to_right_lo = remote(c_hbm.at[lo], mine.at[lo], x_s, x_r, 0, (b, right))
    to_left_hi = remote(c_hbm.at[hi], mine.at[hi], x_s, x_r, 1, (b, left))
    send_k(far)
    send_k(0)
    send_v(0)
    for l in range(levels - 1, far, -1):
        send_k(l)
        send_v(l)
    to_right_hi = remote(c_hbm.at[hi], mine.at[hi], x_s, x_r, 2, (b, right))
    to_left_lo = remote(c_hbm.at[lo], mine.at[lo], x_s, x_r, 3, (b, left))
    sent += [v_mid, to_right_lo, to_left_hi, to_right_hi, to_left_lo]
    for c in loads:
        c.wait()
    kt[...] = k_ref[...].T
    vt[...] = v_ref[...].T

    def own_fwd(h, _):
        for i in range(nb):
            cols = pl.ds(i * STEP, STEP)
            qi = q_ref[cols, hs(h)]
            top = jnp.full((1, STEP), NEG, F32)
            for j in range(i + 1):
                s = mm_t(k_ref[pl.ds(j * STEP, STEP), hs(h)], qi)
                if j == i:
                    key = lax.broadcasted_iota(jnp.int32, (STEP, STEP), 0)
                    query = lax.broadcasted_iota(jnp.int32, (STEP, STEP), 1)
                    s = jnp.where(key <= query, s, NEG)
                s_own[pl.ds(j * STEP, STEP), :] = s
                top = jnp.maximum(top, jnp.max(s, axis=0, keepdims=True))
            m_o[h, :, cols] = top
            total = jnp.zeros((1, STEP), F32)
            part = jnp.zeros((DH, STEP), F32)
            for j in range(i + 1):
                e = jnp.exp2((s_own[pl.ds(j * STEP, STEP), :] - top) * factor)
                total = total + jnp.sum(e, axis=0, keepdims=True)
                e = e.astype(BF16)
                e_own[h, pl.ds(j * STEP, STEP), cols] = e
                part = part + mm(vt[hs(h), pl.ds(j * STEP, STEP)], e)
            l_o[h, :, cols] = total
            acc[hs(h), cols] = part
        return 0

    def forward_tiles():
        ktc[1].wait_recv()
        vtc[1].wait_recv()
        here, there = rows_of(1), rows_of(2)
        ktc[2] = remote(ktile.at[here], ktile.at[there], fwd_s, fwd_r, 4, ahead(1))
        vtc[2] = remote(vtile.at[here], vtile.at[there], fwd_s, fwd_r, 5, ahead(1))
        v_mid.wait_recv()
        vtc[far] = remote(vmid_f, vtile.at[rows_of(far)], fwd_s, fwd_r, 2 * far + 1, end_f)
        sent.extend([ktc[2], vtc[2], vtc[far]])

    own_fwd(0, 0)
    forward_tiles()
    for h in range(1, nh):
        own_fwd(h, 0)

    to_right_lo.wait_recv()
    pass_lo = remote(cot.at[left, lo], cot.at[left, lo], x_s, x_r, 4, (b, right))
    to_left_hi.wait_recv()
    pass_hi = remote(cot.at[right, hi], cot.at[right, hi], x_s, x_r, 5, (b, left))
    sent += [pass_lo, pass_hi]

    for h in range(nh):
        m_t[h] = jnp.full((1, rows), NEG, F32)
    valid = {l: b >= 2**l for l in range(levels)}
    arrive = list(range(levels - 1, far, -1)) + [1, 0, 2, far]
    for l in arrive:
        span = pl.ds(l * TILE, TILE)
        if l != 1:
            ktc[l].wait_recv()
            vtc[l].wait_recv()

        def tile_scores(h, _):
            for i in range(nb):
                cols = pl.ds(i * STEP, STEP)
                s = mm_t(ktile[span, hs(h)], q_ref[cols, hs(h)])
                s_tile[h, span, cols] = s
                top = jnp.max(s, axis=0, keepdims=True)
                m_t[h, :, cols] = jnp.maximum(m_t[h, :, cols], jnp.where(valid[l], top, NEG))
            return 0

        lax.fori_loop(0, nh, tile_scores, 0)
        ktt[:, span] = ktile[span, :].T
        vtt[:, span] = vtile[span, :].T

    def tile_fwd(h, _):
        for i in range(nb):
            cols = pl.ds(i * STEP, STEP)
            top = m_t[h, :, cols]
            total = jnp.zeros((1, STEP), F32)
            part = jnp.zeros((DH, STEP), F32)
            for l in range(levels):
                span = pl.ds(l * TILE, TILE)
                shift = jnp.where(valid[l], top, FAR)
                e = jnp.exp2((s_tile[h, span, cols] - shift) * factor)
                total = total + jnp.sum(e, axis=0, keepdims=True)
                e_tile[h, span, cols] = e.astype(BF16)
            part = mm(vtt[hs(h), :], e_tile[h, :, cols])
            mo = m_o[h, :, cols]
            m = jnp.maximum(mo, top)
            fo = jnp.exp2((mo - m) * factor)
            ft = jnp.exp2((top - m) * factor)
            inv = 1.0 / (fo * l_o[h, :, cols] + ft * total)
            fo = fo * inv
            ft = ft * inv
            r_o[h, :, cols] = fo
            r_t[h, :, cols] = ft
            at = acc[hs(h), cols] * fo + part * ft
            attn_t32[hs(h), cols] = at
            attn_t[hs(h), cols] = at.astype(BF16)
            attn[cols, hs(h)] = at.T.astype(BF16)
        return 0

    lax.fori_loop(0, nh, tile_fwd, 0)

    gh = width // 2
    gy = gh // ny
    gz = heads_x * width // nz
    at_rows = pl.ds(pl.multiple_of(core * gh + yy * gy, gy), gy)
    copies = {}

    def wcols(at):
        return pl.ds(pl.multiple_of(at * width, width), width)

    def yrows(at):
        return pl.ds(pl.multiple_of(at * gy, gy), gy)

    def zcols(at):
        return pl.ds(pl.multiple_of(at * gz, gz), gz)

    def half_rows(at):
        return pl.ds(pl.multiple_of(at * gh, gh), gh)

    def keep(name, *made):
        copies[name] = list(made)
        sent.extend(made)

    def arrived(name):
        for c in copies[name]:
            c.wait_recv()

    def out_over():
        p_send[0] = mm(attn[...], w_ref[:, wcols(over)]).astype(BF16)
        keep("o_lo", remote(p_send.at[0, lo], p_from.at[0, lo], x_s, x_r, 6, (b, right)))
        keep("o_hi", remote(p_send.at[0, hi], p_from.at[1, hi], x_s, x_r, 7, (b, left)))

    def out_next():
        p_send[1] = mm(attn[...], w_ref[:, wcols(right)]).astype(BF16)
        c = remote(p_send.at[1, hi], p_from.at[2, hi], x_s, x_r, 8, (b, right))
        p_send[2] = mm(attn[...], w_ref[:, wcols(left)]).astype(BF16)
        keep("near", c, remote(p_send.at[2, lo], p_from.at[3, lo], x_s, x_r, 9, (b, left)))

    def out_own():
        p_own[...] = mm(attn[...], w_ref[:, wcols(x)])

    def out_pass():
        arrived("o_lo")
        p_send[1, lo, :] = (p_send[1, lo, :].astype(F32) + p_from[0, lo, :].astype(F32)).astype(BF16)
        c = remote(p_send.at[1, lo], p_from.at[2, lo], x_s, x_r, 10, (b, right))
        arrived("o_hi")
        p_send[2, hi, :] = (p_send[2, hi, :].astype(F32) + p_from[1, hi, :].astype(F32)).astype(BF16)
        keep("passed", c, remote(p_send.at[2, hi], p_from.at[3, hi], x_s, x_r, 11, (b, left)))

    def out_end():
        arrived("near")
        arrived("passed")
        out_ref[...] = (p_own[...] + p_from[2].astype(F32) + p_from[3].astype(F32)).astype(BF16)

    def cot_all():
        to_right_hi.wait_recv()
        to_left_lo.wait_recv()
        pass_lo.wait_recv()
        pass_hi.wait_recv()

    def wg_other():
        for j in range(heads_x):
            g_send[:, pl.ds(j * width, width)] = mm(attn_t[half_rows(1 - core), :], cot[j]).astype(BF16)
        keep("core", remote(g_send, g_from, w_s, w_r, 0, sibling))

    def wg_mine():
        for j in range(heads_x):
            g_part[:, pl.ds(j * width, width)] = mm(attn_t[half_rows(core), :], cot[j])

    def wg_y():
        arrived("core")
        g_part[...] = g_part[...] + g_from[...].astype(F32)
        g_ysend[...] = g_part[...].astype(BF16)
        keep("ysum", *[
            remote(g_ysend.at[yrows(ypeer(d))], g_yfrom.at[d], w_s, w_r, d, yid(d)) for d in range(1, ny)
        ])

    def wg_z():
        arrived("ysum")
        total = g_part[yrows(yy), :]
        for d in range(1, ny):
            total = total + g_yfrom[d].astype(F32)
        g_y[...] = total
        g_zsend[...] = total.astype(BF16)
        keep("zsum", *[
            remote(g_zsend.at[:, zcols(zpeer(d))], g_zfrom.at[d], w_s, w_r, ny + d, zid(d))
            for d in range(1, nz)
        ])

    def wg_z_back():
        arrived("zsum")
        piece = g_y[:, zcols(zz)]
        for d in range(1, nz):
            piece = piece + g_zfrom[d].astype(F32)
        own = g_full.at[at_rows, zcols(zz)]
        g_full[at_rows, zcols(zz)] = piece.astype(BF16)
        keep("zall", *[remote(own, own, w_s, w_r, ny + nz + d, zid(d)) for d in range(1, nz)])

    def wg_y_back():
        arrived("zall")
        own = g_full.at[at_rows]
        made = [remote(own, own, w_s, w_r, ny + 2 * nz + d, yid(d)) for d in range(1, ny)]
        made.append(remote(own, own, w_s, w_r, 2 * ny + 2 * nz, sibling))
        keep("yall", *made[:-1])
        keep("last", made[-1])

    def wg_core_back():
        made = []
        for d in range(1, ny):
            copies["yall"][d - 1].wait_recv()
            rows_d = pl.ds(pl.multiple_of(core * gh + lax.rem(yy + ny - d, ny) * gy, gy), gy)
            got = g_full.at[rows_d]
            made.append(remote(got, got, w_s, w_r, 2 * ny + 2 * nz + d, sibling))
        keep("lasts", *made)

    def wg_end():
        arrived("last")
        arrived("lasts")
        wg_ref[...] = g_full[...].astype(F32)

    def dattn():
        for i in range(nb):
            cols = pl.ds(i * STEP, STEP)
            g = jnp.zeros((width, STEP), F32)
            for j in range(heads_x):
                g = g + mm_t(w_ref[:, pl.ds(j * width, width)], cot[j, cols, :])
            datt_t[:, cols] = g.astype(BF16)

    def spread_head(h, _):
        for i in range(nb):
            cols = pl.ds(i * STEP, STEP)
            g = datt_t[hs(h), cols].astype(F32)
            at = attn_t32[hs(h), cols]
            go = (g * r_o[h, :, cols]).astype(BF16)
            gt = (g * r_t[h, :, cols]).astype(BF16)
            datt_o[hs(h), cols] = go
            datt_s[hs(h), cols] = gt
            go = go.astype(F32)
            gt = gt.astype(F32)
            del_o[h, :, cols] = jnp.sum(go * at, axis=0, keepdims=True)
            del_t[h, :, cols] = jnp.sum(gt * at, axis=0, keepdims=True)
            datt_on[cols, hs(h)] = go.T.astype(BF16)
            datt_sn[cols, hs(h)] = gt.T.astype(BF16)
        return 0

    def spread():
        lax.fori_loop(0, nh, spread_head, 0)

    kbc, vbc = {}, {}

    def tile_bwd_for(l):
        span = rows_of(l)

        def tile_bwd(h, _):
            for i in range(nb):
                cols = pl.ds(i * STEP, STEP)
                dp = mm(vtile[span, hs(h)], datt_s[hs(h), cols])
                d = e_tile[h, span, cols].astype(F32) * (dp - del_t[h, :, cols])
                d_tile[h, span, cols] = d.astype(BF16)
            dk = mm(d_tile[h, span, :], q_ref[:, hs(h)]) * scale
            dv = mm(e_tile[h, span, :], datt_sn[:, hs(h)])
            if l == 1:
                one_b[0, :, hs(h)] = dk
                one_b[1, :, hs(h)] = dv
            else:
                ksend[span, hs(h)] = dk.astype(BF16)
                vsend[span, hs(h)] = dv.astype(BF16)
            return 0

        lax.fori_loop(0, nh, tile_bwd, 0)

    def back_k(l, to, dst):
        kbc[l] = remote(ksend.at[rows_of(l)], dst, bwd_s, bwd_r, 2 * l, to)
        sent.append(kbc[l])

    def back_v(l, to, dst):
        vbc[l] = remote(vsend.at[rows_of(l)], dst, bwd_s, bwd_r, 2 * l + 1, to)
        sent.append(vbc[l])

    def tile_two():
        tile_bwd_for(2)
        back_k(2, behind(1), kmid_b)
        back_v(2, behind(1), vmid_b)

    def tile_far():
        tile_bwd_for(far)
        back_v(far, mid_b, vfar_b)
        back_k(far, behind(far), kback.at[rows_of(far)])

    def tile_one():
        tile_bwd_for(1)

    def tile_one_send():
        kbc[2].wait_recv()
        vbc[2].wait_recv()
        ksend[rows_of(1), :] = (one_b[0] + kmid_b[...].astype(F32)).astype(BF16)
        vsend[rows_of(1), :] = (one_b[1] + vmid_b[...].astype(F32)).astype(BF16)
        back_k(1, behind(1), kback.at[rows_of(1)])
        back_v(1, behind(1), vback.at[rows_of(1)])

    def tile_far_pass():
        vbc[far].wait_recv()
        vbc[far] = remote(vfar_b, vback.at[rows_of(far)], bwd_s, bwd_r, 2 * levels, end_b)
        sent.append(vbc[far])

    def tile_direct(l):
        tile_bwd_for(l)
        back_k(l, behind(l), kback.at[rows_of(l)])
        back_v(l, behind(l), vback.at[rows_of(l)])

    def tile_zero():
        tile_direct(0)

    def tile_y():
        for l in range(levels - 1, far, -1):
            tile_direct(l)

    def tile_end():
        dk = dqt[0]
        dv = dqt[1]
        for l in [0, 1, far] + list(range(far + 1, levels)):
            span = rows_of(l)
            kbc[l].wait_recv()
            vbc[l].wait_recv()
            dk = dk + kback[span, :].astype(F32)
            dv = dv + vback[span, :].astype(F32)
        dk_ref[last, :] = dk.astype(BF16)
        dv_ref[last, :] = dv.astype(BF16)

    def own_keys(h, j):
        span = pl.ds(j * STEP, STEP)
        for i in range(j, nb):
            cols = pl.ds(i * STEP, STEP)
            dp = mm(v_ref[span, hs(h)], datt_o[hs(h), cols])
            d = e_own[h, span, cols].astype(F32) * (dp - del_o[h, :, cols])
            d_own[h, span, cols] = d.astype(BF16)
        rest = pl.ds(j * STEP, rows - j * STEP)
        dk = mm(d_own[h, span, rest], q_ref[rest, hs(h)]) * scale
        dv = mm(e_own[h, span, rest], datt_on[rest, hs(h)])
        dk_ref[span, hs(h)] = dk.astype(BF16)
        dv_ref[span, hs(h)] = dv.astype(BF16)
        if j == nb - 1:
            dqt[0, :, hs(h)] = dk[STEP - TILE :]
            dqt[1, :, hs(h)] = dv[STEP - TILE :]

    def own_a():
        for h in range(nh):
            own_keys(h, 0)

    def own_b():
        for h in range(nh):
            for j in range(1, nb):
                own_keys(h, j)

    def own_q():
        for h in range(nh):
            for i in range(nb):
                cols = pl.ds(i * STEP, STEP)
                upto = pl.ds(0, (i + 1) * STEP)
                g = mm(kt[hs(h), upto], d_own[h, upto, cols])
                g = g + mm(ktt[hs(h), :], d_tile[h, :, cols])
                dq_ref[cols, hs(h)] = (g * scale).T.astype(BF16)

    for step in (
cot_all, wg_other, wg_mine, out_over, wg_y, out_next, dattn, spread, own_a, wg_z, tile_two, own_b, wg_z_back, tile_far, tile_zero, tile_one, tile_one_send, wg_y_back, tile_far_pass, tile_y, out_pass, out_own, wg_core_back, own_q, tile_end, wg_end, out_end,
    ):
        step()

    for c in sent:
        c.wait_send()


def local(plan, queries, keys, values, out_weight, cotangent):
    seq, heads_x, levels, ny, nz, _ = plan
    rows, width = queries.shape
    nh = width // DH
    far = levels * TILE
    wide = heads_x * width
    gh = width // 2
    gy = gh // ny
    gz = wide // nz
    dma = pltpu.SemaphoreType.DMA
    like = [(rows, width)] * 4
    return pl.pallas_call(
        functools.partial(kernel, plan),
        out_shape=[pltpu.VMEM(s, BF16) for s in like] + [pltpu.VMEM((width, wide), F32)],
        in_specs=[pl.BlockSpec(memory_space=pl.ANY)] * 5,
        out_specs=[pl.BlockSpec(memory_space=pltpu.VMEM)] * 5,
        scratch_shapes=[
            pltpu.VMEM((rows, width), BF16), pltpu.VMEM((rows, width), BF16),
            pltpu.VMEM((rows, width), BF16), pltpu.VMEM((width, wide), BF16),
            pltpu.VMEM((far, width), BF16), pltpu.VMEM((far, width), BF16),
            pltpu.VMEM((far, width), BF16), pltpu.VMEM((far, width), BF16),
            pltpu.VMEM((far, width), BF16), pltpu.VMEM((far, width), BF16),
            pltpu.VMEM((TILE, width), BF16), pltpu.VMEM((TILE, width), BF16),
            pltpu.VMEM((TILE, width), BF16), pltpu.VMEM((TILE, width), BF16),
            pltpu.VMEM((2, TILE, width), F32),
            pltpu.VMEM((heads_x, rows, width), BF16),
            pltpu.VMEM((width, rows), BF16), pltpu.VMEM((width, rows), BF16),
            pltpu.VMEM((width, far), BF16), pltpu.VMEM((width, far), BF16),
            pltpu.VMEM((rows, STEP), F32), pltpu.VMEM((nh, far, rows), F32),
            pltpu.VMEM((nh, rows, rows), BF16), pltpu.VMEM((nh, far, rows), BF16),
            pltpu.VMEM((nh, rows, rows), BF16), pltpu.VMEM((nh, far, rows), BF16),
            pltpu.VMEM((width, rows), F32), pltpu.VMEM((width, rows), F32),
            pltpu.VMEM((width, rows), BF16), pltpu.VMEM((rows, width), BF16),
        ]
        + [pltpu.VMEM((nh, 1, rows), F32)] * 7
        + [
            pltpu.VMEM((width, rows), BF16), pltpu.VMEM((width, rows), BF16),
            pltpu.VMEM((width, rows), BF16), pltpu.VMEM((rows, width), BF16),
            pltpu.VMEM((rows, width), BF16), pltpu.VMEM((2, TILE, width), F32),
            pltpu.VMEM((3, rows, width), BF16), pltpu.VMEM((rows, width), F32),
            pltpu.VMEM((4, rows, width), BF16),
            pltpu.VMEM((gh, wide), BF16), pltpu.VMEM((gh, wide), BF16),
            pltpu.VMEM((gh, wide), F32), pltpu.VMEM((gh, wide), BF16),
            pltpu.VMEM((ny, gy, wide), BF16), pltpu.VMEM((gy, wide), F32),
            pltpu.VMEM((gy, wide), BF16), pltpu.VMEM((nz, gy, gz), BF16),
            pltpu.VMEM((width, wide), BF16),
            dma((2 * levels + 1,)), dma((2 * levels + 1,)), dma((2 * levels + 1,)), dma((2 * levels + 1,)),
            dma((12,)), dma((12,)),
            dma((3 * ny + 2 * nz,)), dma((3 * ny + 2 * nz,)), dma((5,)),
        ],
        compiler_params=pltpu.CompilerParams(
            collective_id=0, has_side_effects=True, vmem_limit_bytes=52 * 1024 * 1024
        ),
        name="layer",
    )(queries, keys, values, out_weight, cotangent)


def solution(mesh):
    seq = mesh.shape["seq"]
    heads_x = mesh.shape["head"]
    levels = seq.bit_length() - 1
    ny = 4 if seq >= 16 else 2
    ystride = seq // ny
    plan = (seq, heads_x, levels, ny, ystride // 2, ystride)
    return jax.shard_map(
        functools.partial(local, plan),
        mesh=mesh,
        in_specs=(
            P("seq", "head"), P("seq", "head"), P("seq", "head"), P("head", None), P("seq", "head"),
        ),
        out_specs=(
            P("seq", "head"), P("seq", "head"), P("seq", "head"), P("seq", "head"), P("head", None),
        ),
        check_vma=False,
    )
```

```python
import functools

import jax
import jax.numpy as jnp
import numpy as np
from jax import lax
from jax.experimental import pallas as pl
from jax.experimental.pallas import tpu as pltpu
from jax.sharding import PartitionSpec as P

TILE = 128
DH = 128
STEP = 256
MESH = pl.DeviceIdType.MESH
F32 = jnp.float32
BF16 = jnp.bfloat16
NEG = -1e30
FAR = 3e38


def mm(a, b):
    return jnp.dot(a, b, preferred_element_type=F32)


def mm_t(a, b):
    return lax.dot_general(a, b, (((1,), (1,)), ((), ())), preferred_element_type=F32)


def kernel(
    plan,
    q_hbm, k_hbm, v_hbm, w_hbm, c_hbm,
    out_ref, dq_ref, dk_ref, dv_ref, wg_ref,
    q_ref, k_ref, v_ref, w_ref,
    ktile, vtile, kback, vback, ksend, vsend, vmid_f, kmid_b, vmid_b, vfar_b, one_b,
    cot, kt, vt, ktt, vtt,
    s_own, s_tile, e_own, e_tile, d_own, d_tile,
    acc, attn_t32, attn_t, attn, m_o, l_o, m_t, r_o, r_t, del_o, del_t,
    datt_t, datt_o, datt_s, datt_on, datt_sn, dqt,
    p_send, p_own, p_from,
    g_send, g_from, g_part, g_ysend, g_yfrom, g_y, g_zsend, g_zfrom, g_full,
    fwd_s, fwd_r, bwd_s, bwd_r, x_s, x_r, w_s, w_r, in_s,
):
    seq, heads_x, levels, ny, nz, ystride = plan
    rows, width = q_hbm.shape
    nh = width // DH
    nb = rows // STEP
    tail = rows - TILE
    b = lax.axis_index("seq")
    x = lax.axis_index("head")
    core = lax.rem(b, 2)
    yy = b // ystride
    zz = lax.rem(b, ystride) // 2
    right = lax.rem(x + 1, heads_x)
    left = lax.rem(x + heads_x - 1, heads_x)
    over = lax.rem(x + 2, heads_x)
    far = levels // 2
    factor = float(DH ** (-0.5) * np.log2(np.e))
    scale = DH ** (-0.5)

    def ahead(l):
        return (lax.rem(b + 2**l, seq), x)

    def behind(l):
        return (lax.rem(b + seq - 2**l, seq), x)

    sibling = (b + 1 - 2 * core, x)

    def ypeer(d):
        return lax.rem(yy + d, ny)

    def zpeer(d):
        return lax.rem(zz + d, nz)

    def yid(d):
        return (ypeer(d) * ystride + zz * 2 + core, x)

    def zid(d):
        return (yy * ystride + zpeer(d) * 2 + core, x)

    def from_z(dz):
        return yy * ystride + lax.rem(zz + dz + nz, nz) * 2 + core

    reach = 2**far
    mid_f = (from_z(-2), x)
    mid_b = (from_z(2), x)
    end_f = (lax.rem(from_z(2) + reach, seq), x)
    end_b = (lax.rem(from_z(-2) - reach + seq, seq), x)
    src_f, src_b = lax.rem(b + seq - reach, seq), lax.rem(b + reach, seq)
    pass_f = (src_f // ystride * ystride + lax.rem(lax.rem(src_f, ystride) // 2 + nz - 2, nz) * 2 + core, x)
    pass_b = (src_b // ystride * ystride + lax.rem(lax.rem(src_b, ystride) // 2 + 2, nz) * 2 + core, x)

    peers = [behind(0), ahead(0), behind(1), ahead(1), behind(far), ahead(far), pass_f, pass_b]
    peers += [yid(d) for d in range(1, ny)] + [zid(d) for d in range(1, nz)]
    peers += [(b, right), (b, left)]
    barrier = pltpu.get_barrier_semaphore()
    for peer in peers:
        pl.semaphore_signal(barrier, inc=1, device_id=peer, device_id_type=MESH)

    def remote(src, dst, sems, semr, idx, to):
        c = pltpu.make_async_remote_copy(
            src_ref=src, dst_ref=dst, send_sem=sems.at[idx], recv_sem=semr.at[idx],
            device_id=to, device_id_type=MESH,
        )
        c.start()
        return c

    def hs(h):
        return pl.ds(pl.multiple_of(h * DH, DH), DH)

    loads = [
        pltpu.make_async_copy(src, dst, in_s.at[n])
        for n, (src, dst) in enumerate(
            [(k_hbm, k_ref), (v_hbm, v_ref), (q_hbm, q_ref), (c_hbm, cot.at[x]), (w_hbm, w_ref)]
        )
    ]
    for c in loads:
        c.start()
    pl.semaphore_wait(barrier, len(peers))

    def rows_of(l):
        return pl.ds(l * TILE, TILE)

    sent = []
    ktc, vtc = {}, {}
    last = pl.ds(tail, TILE)

    def send_k(l):
        ktc[l] = remote(k_hbm.at[last], ktile.at[rows_of(l)], fwd_s, fwd_r, 2 * l, ahead(l))
        sent.append(ktc[l])

    def send_v(l):
        vtc[l] = remote(v_hbm.at[last], vtile.at[rows_of(l)], fwd_s, fwd_r, 2 * l + 1, ahead(l))
        sent.append(vtc[l])

    half = rows // 2
    lo, hi = pl.ds(0, half), pl.ds(half, half)
    mine = cot.at[x]
    send_k(1)
    send_v(1)
    v_mid = remote(v_hbm.at[last], vmid_f, fwd_s, fwd_r, 2 * levels, mid_f)
    to_right_lo = remote(c_hbm.at[lo], mine.at[lo], x_s, x_r, 0, (b, right))
    to_left_hi = remote(c_hbm.at[hi], mine.at[hi], x_s, x_r, 1, (b, left))
    send_k(far)
    send_k(0)
    send_v(0)
    for l in range(levels - 1, far, -1):
        send_k(l)
        send_v(l)
    to_right_hi = remote(c_hbm.at[hi], mine.at[hi], x_s, x_r, 2, (b, right))
    to_left_lo = remote(c_hbm.at[lo], mine.at[lo], x_s, x_r, 3, (b, left))
    sent += [v_mid, to_right_lo, to_left_hi, to_right_hi, to_left_lo]
    for c in loads:
        c.wait()
    kt[...] = k_ref[...].T
    vt[...] = v_ref[...].T

    def own_fwd(h, _):
        for i in range(nb):
            cols = pl.ds(i * STEP, STEP)
            qi = q_ref[cols, hs(h)]
            top = jnp.full((1, STEP), NEG, F32)
            for j in range(i + 1):
                s = mm_t(k_ref[pl.ds(j * STEP, STEP), hs(h)], qi)
                if j == i:
                    key = lax.broadcasted_iota(jnp.int32, (STEP, STEP), 0)
                    query = lax.broadcasted_iota(jnp.int32, (STEP, STEP), 1)
                    s = jnp.where(key <= query, s, NEG)
                s_own[pl.ds(j * STEP, STEP), :] = s
                top = jnp.maximum(top, jnp.max(s, axis=0, keepdims=True))
            m_o[h, :, cols] = top
            total = jnp.zeros((1, STEP), F32)
            part = jnp.zeros((DH, STEP), F32)
            for j in range(i + 1):
                e = jnp.exp2((s_own[pl.ds(j * STEP, STEP), :] - top) * factor)
                total = total + jnp.sum(e, axis=0, keepdims=True)
                e = e.astype(BF16)
                e_own[h, pl.ds(j * STEP, STEP), cols] = e
                part = part + mm(vt[hs(h), pl.ds(j * STEP, STEP)], e)
            l_o[h, :, cols] = total
            acc[hs(h), cols] = part
        return 0

    def forward_tiles():
        ktc[1].wait_recv()
        vtc[1].wait_recv()
        here, there = rows_of(1), rows_of(2)
        ktc[2] = remote(ktile.at[here], ktile.at[there], fwd_s, fwd_r, 4, ahead(1))
        vtc[2] = remote(vtile.at[here], vtile.at[there], fwd_s, fwd_r, 5, ahead(1))
        v_mid.wait_recv()
        vtc[far] = remote(vmid_f, vtile.at[rows_of(far)], fwd_s, fwd_r, 2 * far + 1, end_f)
        sent.extend([ktc[2], vtc[2], vtc[far]])

    own_fwd(0, 0)
    forward_tiles()
    for h in range(1, nh):
        own_fwd(h, 0)

    to_right_lo.wait_recv()
    pass_lo = remote(cot.at[left, lo], cot.at[left, lo], x_s, x_r, 4, (b, right))
    to_left_hi.wait_recv()
    pass_hi = remote(cot.at[right, hi], cot.at[right, hi], x_s, x_r, 5, (b, left))
    sent += [pass_lo, pass_hi]

    for h in range(nh):
        m_t[h] = jnp.full((1, rows), NEG, F32)
    valid = {l: b >= 2**l for l in range(levels)}
    for pair in (levels - 2, 0, far - 1):
        span = pl.ds(pair * TILE, 2 * TILE)
        for l in (pair, pair + 1):
            if l != 1:
                ktc[l].wait_recv()
                vtc[l].wait_recv()

        def tile_scores(h, _):
            for i in range(nb):
                cols = pl.ds(i * STEP, STEP)
                s = mm_t(ktile[span, hs(h)], q_ref[cols, hs(h)])
                s_tile[h, span, cols] = s
                top = jnp.max(s[:TILE], axis=0, keepdims=True)
                second = jnp.max(s[TILE:], axis=0, keepdims=True)
                top = jnp.where(valid[pair], top, NEG)
                second = jnp.where(valid[pair + 1], second, NEG)
                m_t[h, :, cols] = jnp.maximum(m_t[h, :, cols], jnp.maximum(top, second))
            return 0

        lax.fori_loop(0, nh, tile_scores, 0)
        ktt[:, span] = ktile[span, :].T
        vtt[:, span] = vtile[span, :].T

    def tile_fwd(h, _):
        for i in range(nb):
            cols = pl.ds(i * STEP, STEP)
            top = m_t[h, :, cols]
            total = jnp.zeros((1, STEP), F32)
            part = jnp.zeros((DH, STEP), F32)
            for l in range(levels):
                span = pl.ds(l * TILE, TILE)
                shift = jnp.where(valid[l], top, FAR)
                e = jnp.exp2((s_tile[h, span, cols] - shift) * factor)
                total = total + jnp.sum(e, axis=0, keepdims=True)
                e_tile[h, span, cols] = e.astype(BF16)
            part = mm(vtt[hs(h), :], e_tile[h, :, cols])
            mo = m_o[h, :, cols]
            m = jnp.maximum(mo, top)
            fo = jnp.exp2((mo - m) * factor)
            ft = jnp.exp2((top - m) * factor)
            inv = 1.0 / (fo * l_o[h, :, cols] + ft * total)
            fo = fo * inv
            ft = ft * inv
            r_o[h, :, cols] = fo
            r_t[h, :, cols] = ft
            at = acc[hs(h), cols] * fo + part * ft
            attn_t32[hs(h), cols] = at
            attn_t[hs(h), cols] = at.astype(BF16)
            attn[cols, hs(h)] = at.T.astype(BF16)
        return 0

    lax.fori_loop(0, nh, tile_fwd, 0)

    gh = width // 2
    gy = gh // ny
    gz = heads_x * width // nz
    at_rows = pl.ds(pl.multiple_of(core * gh + yy * gy, gy), gy)
    copies = {}

    def wcols(at):
        return pl.ds(pl.multiple_of(at * width, width), width)

    def yrows(at):
        return pl.ds(pl.multiple_of(at * gy, gy), gy)

    def zcols(at):
        return pl.ds(pl.multiple_of(at * gz, gz), gz)

    def half_rows(at):
        return pl.ds(pl.multiple_of(at * gh, gh), gh)

    def keep(name, *made):
        copies[name] = list(made)
        sent.extend(made)

    def arrived(name):
        for c in copies[name]:
            c.wait_recv()

    def out_over():
        p_send[0] = mm(attn[...], w_ref[:, wcols(over)]).astype(BF16)
        keep("o_lo", remote(p_send.at[0, lo], p_from.at[0, lo], x_s, x_r, 6, (b, right)))
        keep("o_hi", remote(p_send.at[0, hi], p_from.at[1, hi], x_s, x_r, 7, (b, left)))

    def out_next():
        p_send[1] = mm(attn[...], w_ref[:, wcols(right)]).astype(BF16)
        c = remote(p_send.at[1, hi], p_from.at[2, hi], x_s, x_r, 8, (b, right))
        p_send[2] = mm(attn[...], w_ref[:, wcols(left)]).astype(BF16)
        keep("near", c, remote(p_send.at[2, lo], p_from.at[3, lo], x_s, x_r, 9, (b, left)))

    def out_own():
        p_own[...] = mm(attn[...], w_ref[:, wcols(x)])

    def out_pass():
        arrived("o_lo")
        p_send[1, lo, :] = (p_send[1, lo, :].astype(F32) + p_from[0, lo, :].astype(F32)).astype(BF16)
        c = remote(p_send.at[1, lo], p_from.at[2, lo], x_s, x_r, 10, (b, right))
        arrived("o_hi")
        p_send[2, hi, :] = (p_send[2, hi, :].astype(F32) + p_from[1, hi, :].astype(F32)).astype(BF16)
        keep("passed", c, remote(p_send.at[2, hi], p_from.at[3, hi], x_s, x_r, 11, (b, left)))

    def out_end():
        arrived("near")
        arrived("passed")
        out_ref[...] = (p_own[...] + p_from[2].astype(F32) + p_from[3].astype(F32)).astype(BF16)

    def cot_all():
        to_right_hi.wait_recv()
        to_left_lo.wait_recv()
        pass_lo.wait_recv()
        pass_hi.wait_recv()

    def wg_other():
        for j in range(heads_x):
            g_send[:, pl.ds(j * width, width)] = mm(attn_t[half_rows(1 - core), :], cot[j]).astype(BF16)
        keep("core", remote(g_send, g_from, w_s, w_r, 0, sibling))

    def wg_mine():
        for j in range(heads_x):
            g_part[:, pl.ds(j * width, width)] = mm(attn_t[half_rows(core), :], cot[j])

    def wg_y():
        arrived("core")
        g_part[...] = g_part[...] + g_from[...].astype(F32)
        g_ysend[...] = g_part[...].astype(BF16)
        keep("ysum", *[
            remote(g_ysend.at[yrows(ypeer(d))], g_yfrom.at[d], w_s, w_r, d, yid(d)) for d in range(1, ny)
        ])

    def wg_z():
        arrived("ysum")
        total = g_part[yrows(yy), :]
        for d in range(1, ny):
            total = total + g_yfrom[d].astype(F32)
        g_y[...] = total
        g_zsend[...] = total.astype(BF16)
        keep("zsum", *[
            remote(g_zsend.at[:, zcols(zpeer(d))], g_zfrom.at[d], w_s, w_r, ny + d, zid(d))
            for d in range(1, nz)
        ])

    def wg_z_back():
        arrived("zsum")
        piece = g_y[:, zcols(zz)]
        for d in range(1, nz):
            piece = piece + g_zfrom[d].astype(F32)
        own = g_full.at[at_rows, zcols(zz)]
        g_full[at_rows, zcols(zz)] = piece.astype(BF16)
        keep("zall", *[remote(own, own, w_s, w_r, ny + nz + d, zid(d)) for d in range(1, nz)])

    def wg_y_back():
        arrived("zall")
        own = g_full.at[at_rows]
        made = [remote(own, own, w_s, w_r, ny + 2 * nz + d, yid(d)) for d in range(1, ny)]
        made.append(remote(own, own, w_s, w_r, 2 * ny + 2 * nz, sibling))
        keep("yall", *made[:-1])
        keep("last", made[-1])

    def wg_core_back():
        made = []
        for d in range(1, ny):
            copies["yall"][d - 1].wait_recv()
            rows_d = pl.ds(pl.multiple_of(core * gh + lax.rem(yy + ny - d, ny) * gy, gy), gy)
            got = g_full.at[rows_d]
            made.append(remote(got, got, w_s, w_r, 2 * ny + 2 * nz + d, sibling))
        keep("lasts", *made)

    def wg_end():
        arrived("last")
        arrived("lasts")
        wg_ref[...] = g_full[...].astype(F32)

    def dattn():
        for i in range(nb):
            cols = pl.ds(i * STEP, STEP)
            g = jnp.zeros((width, STEP), F32)
            for j in range(heads_x):
                g = g + mm_t(w_ref[:, pl.ds(j * width, width)], cot[j, cols, :])
            datt_t[:, cols] = g.astype(BF16)

    def spread_head(h, _):
        for i in range(nb):
            cols = pl.ds(i * STEP, STEP)
            g = datt_t[hs(h), cols].astype(F32)
            at = attn_t32[hs(h), cols]
            go = (g * r_o[h, :, cols]).astype(BF16)
            gt = (g * r_t[h, :, cols]).astype(BF16)
            datt_o[hs(h), cols] = go
            datt_s[hs(h), cols] = gt
            go = go.astype(F32)
            gt = gt.astype(F32)
            del_o[h, :, cols] = jnp.sum(go * at, axis=0, keepdims=True)
            del_t[h, :, cols] = jnp.sum(gt * at, axis=0, keepdims=True)
            datt_on[cols, hs(h)] = go.T.astype(BF16)
            datt_sn[cols, hs(h)] = gt.T.astype(BF16)
        return 0

    def spread():
        lax.fori_loop(0, nh, spread_head, 0)

    kbc, vbc = {}, {}

    def tile_bwd_for(pair):
        span = pl.ds(pair * TILE, 2 * TILE)

        def tile_bwd(h, _):
            for i in range(nb):
                cols = pl.ds(i * STEP, STEP)
                dp = mm(vtile[span, hs(h)], datt_s[hs(h), cols])
                d = e_tile[h, span, cols].astype(F32) * (dp - del_t[h, :, cols])
                d_tile[h, span, cols] = d.astype(BF16)
            dk = mm(d_tile[h, span, :], q_ref[:, hs(h)]) * scale
            dv = mm(e_tile[h, span, :], datt_sn[:, hs(h)])
            if pair == 0:
                one_b[0, :, hs(h)] = dk[TILE:]
                one_b[1, :, hs(h)] = dv[TILE:]
            ksend[span, hs(h)] = dk.astype(BF16)
            vsend[span, hs(h)] = dv.astype(BF16)
            return 0

        lax.fori_loop(0, nh, tile_bwd, 0)

    def back_k(l, to, dst):
        kbc[l] = remote(ksend.at[rows_of(l)], dst, bwd_s, bwd_r, 2 * l, to)
        sent.append(kbc[l])

    def back_v(l, to, dst):
        vbc[l] = remote(vsend.at[rows_of(l)], dst, bwd_s, bwd_r, 2 * l + 1, to)
        sent.append(vbc[l])

    def tile_z():
        tile_bwd_for(far - 1)
        back_k(2, behind(1), kmid_b)
        back_v(2, behind(1), vmid_b)
        back_v(far, mid_b, vfar_b)
        back_k(far, behind(far), kback.at[rows_of(far)])

    def tile_near():
        tile_bwd_for(0)
        tile_direct(0)

    def tile_one_send():
        kbc[2].wait_recv()
        vbc[2].wait_recv()
        ksend[rows_of(1), :] = (one_b[0] + kmid_b[...].astype(F32)).astype(BF16)
        vsend[rows_of(1), :] = (one_b[1] + vmid_b[...].astype(F32)).astype(BF16)
        back_k(1, behind(1), kback.at[rows_of(1)])
        back_v(1, behind(1), vback.at[rows_of(1)])

    def tile_far_pass():
        vbc[far].wait_recv()
        vbc[far] = remote(vfar_b, vback.at[rows_of(far)], bwd_s, bwd_r, 2 * levels, end_b)
        sent.append(vbc[far])

    def tile_direct(l):
        back_k(l, behind(l), kback.at[rows_of(l)])
        back_v(l, behind(l), vback.at[rows_of(l)])

    def tile_y():
        tile_bwd_for(levels - 2)
        for l in range(levels - 1, far, -1):
            tile_direct(l)

    def tile_end():
        dk = dqt[0]
        dv = dqt[1]
        for l in [0, 1, far] + list(range(far + 1, levels)):
            span = rows_of(l)
            kbc[l].wait_recv()
            vbc[l].wait_recv()
            dk = dk + kback[span, :].astype(F32)
            dv = dv + vback[span, :].astype(F32)
        dk_ref[last, :] = dk.astype(BF16)
        dv_ref[last, :] = dv.astype(BF16)

    def own_keys(h, j):
        span = pl.ds(j * STEP, STEP)
        for i in range(j, nb):
            cols = pl.ds(i * STEP, STEP)
            dp = mm(v_ref[span, hs(h)], datt_o[hs(h), cols])
            d = e_own[h, span, cols].astype(F32) * (dp - del_o[h, :, cols])
            d_own[h, span, cols] = d.astype(BF16)
        rest = pl.ds(j * STEP, rows - j * STEP)
        dk = mm(d_own[h, span, rest], q_ref[rest, hs(h)]) * scale
        dv = mm(e_own[h, span, rest], datt_on[rest, hs(h)])
        dk_ref[span, hs(h)] = dk.astype(BF16)
        dv_ref[span, hs(h)] = dv.astype(BF16)
        if j == nb - 1:
            dqt[0, :, hs(h)] = dk[STEP - TILE :]
            dqt[1, :, hs(h)] = dv[STEP - TILE :]

    def own_a():
        for h in range(nh):
            own_keys(h, 0)

    def own_b():
        for h in range(nh):
            for j in range(1, nb):
                own_keys(h, j)

    def own_q():
        for h in range(nh):
            for i in range(nb):
                cols = pl.ds(i * STEP, STEP)
                upto = pl.ds(0, (i + 1) * STEP)
                g = mm(kt[hs(h), upto], d_own[h, upto, cols])
                g = g + mm(ktt[hs(h), :], d_tile[h, :, cols])
                dq_ref[cols, hs(h)] = (g * scale).T.astype(BF16)

    for step in (
cot_all, wg_other, wg_mine, out_over, wg_y, out_next, dattn, spread, own_a, wg_z, tile_z, tile_near, wg_z_back, tile_one_send, wg_y_back, tile_far_pass, tile_y, own_b, out_pass, out_own, wg_core_back, own_q, wg_end, tile_end, out_end,
    ):
        step()

    for c in sent:
        c.wait_send()


def store(*refs):
    n = len(refs) // 2
    made = [pltpu.make_async_copy(refs[i], refs[n + i], refs[-1].at[i]) for i in range(n)]
    for c in made:
        c.start()
    for c in made:
        c.wait()


def local(plan, queries, keys, values, out_weight, cotangent):
    seq, heads_x, levels, ny, nz, _ = plan
    rows, width = queries.shape
    nh = width // DH
    far = levels * TILE
    wide = heads_x * width
    gh = width // 2
    gy = gh // ny
    gz = wide // nz
    dma = pltpu.SemaphoreType.DMA
    like = [(rows, width)] * 4
    shapes = [jax.ShapeDtypeStruct(s, BF16) for s in like] + [jax.ShapeDtypeStruct((width, wide), F32)]
    made = pl.pallas_call(
        functools.partial(kernel, plan),
        out_shape=[pltpu.VMEM(s, BF16) for s in like] + [pltpu.VMEM((width, wide), F32)],
        in_specs=[pl.BlockSpec(memory_space=pl.ANY)] * 5,
        out_specs=[pl.BlockSpec(memory_space=pltpu.VMEM)] * 5,
        scratch_shapes=[
            pltpu.VMEM((rows, width), BF16), pltpu.VMEM((rows, width), BF16),
            pltpu.VMEM((rows, width), BF16), pltpu.VMEM((width, wide), BF16),
            pltpu.VMEM((far, width), BF16), pltpu.VMEM((far, width), BF16),
            pltpu.VMEM((far, width), BF16), pltpu.VMEM((far, width), BF16),
            pltpu.VMEM((far, width), BF16), pltpu.VMEM((far, width), BF16),
            pltpu.VMEM((TILE, width), BF16), pltpu.VMEM((TILE, width), BF16),
            pltpu.VMEM((TILE, width), BF16), pltpu.VMEM((TILE, width), BF16),
            pltpu.VMEM((2, TILE, width), F32),
            pltpu.VMEM((heads_x, rows, width), BF16),
            pltpu.VMEM((width, rows), BF16), pltpu.VMEM((width, rows), BF16),
            pltpu.VMEM((width, far), BF16), pltpu.VMEM((width, far), BF16),
            pltpu.VMEM((rows, STEP), F32), pltpu.VMEM((nh, far, rows), F32),
            pltpu.VMEM((nh, rows, rows), BF16), pltpu.VMEM((nh, far, rows), BF16),
            pltpu.VMEM((nh, rows, rows), BF16), pltpu.VMEM((nh, far, rows), BF16),
            pltpu.VMEM((width, rows), F32), pltpu.VMEM((width, rows), F32),
            pltpu.VMEM((width, rows), BF16), pltpu.VMEM((rows, width), BF16),
        ]
        + [pltpu.VMEM((nh, 1, rows), F32)] * 7
        + [
            pltpu.VMEM((width, rows), BF16), pltpu.VMEM((width, rows), BF16),
            pltpu.VMEM((width, rows), BF16), pltpu.VMEM((rows, width), BF16),
            pltpu.VMEM((rows, width), BF16), pltpu.VMEM((2, TILE, width), F32),
            pltpu.VMEM((3, rows, width), BF16), pltpu.VMEM((rows, width), F32),
            pltpu.VMEM((4, rows, width), BF16),
            pltpu.VMEM((gh, wide), BF16), pltpu.VMEM((gh, wide), BF16),
            pltpu.VMEM((gh, wide), F32), pltpu.VMEM((gh, wide), BF16),
            pltpu.VMEM((ny, gy, wide), BF16), pltpu.VMEM((gy, wide), F32),
            pltpu.VMEM((gy, wide), BF16), pltpu.VMEM((nz, gy, gz), BF16),
            pltpu.VMEM((width, wide), BF16),
            dma((2 * levels + 1,)), dma((2 * levels + 1,)), dma((2 * levels + 1,)), dma((2 * levels + 1,)),
            dma((12,)), dma((12,)),
            dma((3 * ny + 2 * nz,)), dma((3 * ny + 2 * nz,)), dma((5,)),
        ],
        compiler_params=pltpu.CompilerParams(
            collective_id=0, has_side_effects=True, vmem_limit_bytes=52 * 1024 * 1024
        ),
        name="layer",
    )(queries, keys, values, out_weight, cotangent)
    return pl.pallas_call(
        store,
        out_shape=shapes,
        in_specs=[pl.BlockSpec(memory_space=pltpu.VMEM)] * 5,
        out_specs=[pl.BlockSpec(memory_space=pl.ANY)] * 5,
        scratch_shapes=[dma((5,))],
        name="store",
    )(*[pltpu.with_memory_space_constraint(a, pltpu.VMEM) for a in made])


def solution(mesh):
    seq = mesh.shape["seq"]
    heads_x = mesh.shape["head"]
    levels = seq.bit_length() - 1
    ny = 4 if seq >= 16 else 2
    ystride = seq // ny
    plan = (seq, heads_x, levels, ny, ystride // 2, ystride)
    return jax.shard_map(
        functools.partial(local, plan),
        mesh=mesh,
        in_specs=(
            P("seq", "head"), P("seq", "head"), P("seq", "head"), P("head", None), P("seq", "head"),
        ),
        out_specs=(
            P("seq", "head"), P("seq", "head"), P("seq", "head"), P("seq", "head"), P("head", None),
        ),
        check_vma=False,
    )
```

```python
import functools

import jax
import jax.numpy as jnp
import numpy as np
from jax import lax
from jax.experimental import pallas as pl
from jax.experimental.pallas import tpu as pltpu
from jax.sharding import PartitionSpec as P

TILE = 128
DH = 128
STEP = 256
MESH = pl.DeviceIdType.MESH
F32 = jnp.float32
BF16 = jnp.bfloat16
NEG = -1e30
FAR = 3e38


def mm(a, b):
    return jnp.dot(a, b, preferred_element_type=F32)


def mm_t(a, b):
    return lax.dot_general(a, b, (((1,), (1,)), ((), ())), preferred_element_type=F32)


def kernel(
    plan,
    q_hbm, k_hbm, v_hbm, w_hbm, c_hbm,
    out_ref, dq_ref, dk_ref, dv_ref, wg_ref,
    q_ref, k_ref, v_ref, w_ref,
    ktile, vtile, kback, vback, ksend, vsend, vmid_f, kmid_b, vmid_b, vfar_b, one_b,
    cot, kt, vt, ktt, vtt,
    s_own, s_tile, e_own, e_tile, d_own, d_tile,
    acc, attn_t32, attn_t, attn, m_o, l_o, m_t, r_o, r_t, del_o, del_t,
    datt_t, datt_o, datt_s, datt_on, datt_sn, dqt,
    p_send, p_own, p_from,
    g_send, g_from, g_part, g_ysend, g_yfrom, g_y, g_zsend, g_zfrom, g_full,
    fwd_s, fwd_r, bwd_s, bwd_r, x_s, x_r, w_s, w_r, in_s,
):
    seq, heads_x, levels, ny, nz, ystride = plan
    rows, width = q_hbm.shape
    nh = width // DH
    nb = rows // STEP
    tail = rows - TILE
    b = lax.axis_index("seq")
    x = lax.axis_index("head")
    core = lax.rem(b, 2)
    yy = b // ystride
    zz = lax.rem(b, ystride) // 2
    right = lax.rem(x + 1, heads_x)
    left = lax.rem(x + heads_x - 1, heads_x)
    over = lax.rem(x + 2, heads_x)
    far = levels // 2
    factor = float(DH ** (-0.5) * np.log2(np.e))
    scale = DH ** (-0.5)

    def ahead(l):
        return (lax.rem(b + 2**l, seq), x)

    def behind(l):
        return (lax.rem(b + seq - 2**l, seq), x)

    sibling = (b + 1 - 2 * core, x)

    def ypeer(d):
        return lax.rem(yy + d, ny)

    def zpeer(d):
        return lax.rem(zz + d, nz)

    def yid(d):
        return (ypeer(d) * ystride + zz * 2 + core, x)

    def zid(d):
        return (yy * ystride + zpeer(d) * 2 + core, x)

    def from_z(dz):
        return yy * ystride + lax.rem(zz + dz + nz, nz) * 2 + core

    reach = 2**far
    mid_f = (from_z(-2), x)
    mid_b = (from_z(2), x)
    end_f = (lax.rem(from_z(2) + reach, seq), x)
    end_b = (lax.rem(from_z(-2) - reach + seq, seq), x)
    src_f, src_b = lax.rem(b + seq - reach, seq), lax.rem(b + reach, seq)
    pass_f = (src_f // ystride * ystride + lax.rem(lax.rem(src_f, ystride) // 2 + nz - 2, nz) * 2 + core, x)
    pass_b = (src_b // ystride * ystride + lax.rem(lax.rem(src_b, ystride) // 2 + 2, nz) * 2 + core, x)

    peers = [behind(0), ahead(0), behind(1), ahead(1), behind(far), ahead(far), pass_f, pass_b]
    peers += [yid(d) for d in range(1, ny)] + [zid(d) for d in range(1, nz)]
    peers += [(b, right), (b, left)]
    barrier = pltpu.get_barrier_semaphore()
    for peer in peers:
        pl.semaphore_signal(barrier, inc=1, device_id=peer, device_id_type=MESH)

    def remote(src, dst, sems, semr, idx, to):
        c = pltpu.make_async_remote_copy(
            src_ref=src, dst_ref=dst, send_sem=sems.at[idx], recv_sem=semr.at[idx],
            device_id=to, device_id_type=MESH,
        )
        c.start()
        return c

    def hs(h):
        return pl.ds(pl.multiple_of(h * DH, DH), DH)

    loads = [
        pltpu.make_async_copy(src, dst, in_s.at[n])
        for n, (src, dst) in enumerate(
            [(k_hbm, k_ref), (v_hbm, v_ref), (q_hbm, q_ref), (c_hbm, cot.at[x]), (w_hbm, w_ref)]
        )
    ]
    for c in loads:
        c.start()
    pl.semaphore_wait(barrier, len(peers))

    def rows_of(l):
        return pl.ds(l * TILE, TILE)

    sent = []
    ktc, vtc = {}, {}
    last = pl.ds(tail, TILE)

    def send_k(l):
        ktc[l] = remote(k_hbm.at[last], ktile.at[rows_of(l)], fwd_s, fwd_r, 2 * l, ahead(l))
        sent.append(ktc[l])

    def send_v(l):
        vtc[l] = remote(v_hbm.at[last], vtile.at[rows_of(l)], fwd_s, fwd_r, 2 * l + 1, ahead(l))
        sent.append(vtc[l])

    half = rows // 2
    lo, hi = pl.ds(0, half), pl.ds(half, half)
    mine = cot.at[x]
    send_k(1)
    send_v(1)
    v_mid = remote(v_hbm.at[last], vmid_f, fwd_s, fwd_r, 2 * levels, mid_f)
    to_right_lo = remote(c_hbm.at[lo], mine.at[lo], x_s, x_r, 0, (b, right))
    to_left_hi = remote(c_hbm.at[hi], mine.at[hi], x_s, x_r, 1, (b, left))
    send_k(far)
    send_k(0)
    send_v(0)
    for l in range(levels - 1, far, -1):
        send_k(l)
        send_v(l)
    to_right_hi = remote(c_hbm.at[hi], mine.at[hi], x_s, x_r, 2, (b, right))
    to_left_lo = remote(c_hbm.at[lo], mine.at[lo], x_s, x_r, 3, (b, left))
    sent += [v_mid, to_right_lo, to_left_hi, to_right_hi, to_left_lo]
    for c in loads:
        c.wait()
    kt[...] = k_ref[...].T
    vt[...] = v_ref[...].T

    def own_fwd(h, _):
        for i in range(nb):
            cols = pl.ds(i * STEP, STEP)
            qi = q_ref[cols, hs(h)]
            top = jnp.full((1, STEP), NEG, F32)
            for j in range(i + 1):
                s = mm_t(k_ref[pl.ds(j * STEP, STEP), hs(h)], qi)
                if j == i:
                    key = lax.broadcasted_iota(jnp.int32, (STEP, STEP), 0)
                    query = lax.broadcasted_iota(jnp.int32, (STEP, STEP), 1)
                    s = jnp.where(key <= query, s, NEG)
                s_own[pl.ds(j * STEP, STEP), :] = s
                top = jnp.maximum(top, jnp.max(s, axis=0, keepdims=True))
            m_o[h, :, cols] = top
            total = jnp.zeros((1, STEP), F32)
            part = jnp.zeros((DH, STEP), F32)
            for j in range(i + 1):
                e = jnp.exp2((s_own[pl.ds(j * STEP, STEP), :] - top) * factor)
                total = total + jnp.sum(e, axis=0, keepdims=True)
                e = e.astype(BF16)
                e_own[h, pl.ds(j * STEP, STEP), cols] = e
                part = part + mm(vt[hs(h), pl.ds(j * STEP, STEP)], e)
            l_o[h, :, cols] = total
            acc[hs(h), cols] = part
        return 0

    def forward_tiles():
        ktc[1].wait_recv()
        vtc[1].wait_recv()
        here, there = rows_of(1), rows_of(2)
        ktc[2] = remote(ktile.at[here], ktile.at[there], fwd_s, fwd_r, 4, ahead(1))
        vtc[2] = remote(vtile.at[here], vtile.at[there], fwd_s, fwd_r, 5, ahead(1))
        v_mid.wait_recv()
        vtc[far] = remote(vmid_f, vtile.at[rows_of(far)], fwd_s, fwd_r, 2 * far + 1, end_f)
        sent.extend([ktc[2], vtc[2], vtc[far]])

    own_fwd(0, 0)
    forward_tiles()
    for h in range(1, nh):
        own_fwd(h, 0)

    to_right_lo.wait_recv()
    pass_lo = remote(cot.at[left, lo], cot.at[left, lo], x_s, x_r, 4, (b, right))
    to_left_hi.wait_recv()
    pass_hi = remote(cot.at[right, hi], cot.at[right, hi], x_s, x_r, 5, (b, left))
    sent += [pass_lo, pass_hi]

    for h in range(nh):
        m_t[h] = jnp.full((1, rows), NEG, F32)
    valid = {l: b >= 2**l for l in range(levels)}
    for pair in (levels - 2, 0, far - 1):
        span = pl.ds(pair * TILE, 2 * TILE)
        for l in (pair, pair + 1):
            if l != 1:
                ktc[l].wait_recv()
                vtc[l].wait_recv()

        def tile_scores(h, _):
            for i in range(nb):
                cols = pl.ds(i * STEP, STEP)
                s = mm_t(ktile[span, hs(h)], q_ref[cols, hs(h)])
                s_tile[h, span, cols] = s
                top = jnp.max(s[:TILE], axis=0, keepdims=True)
                second = jnp.max(s[TILE:], axis=0, keepdims=True)
                top = jnp.where(valid[pair], top, NEG)
                second = jnp.where(valid[pair + 1], second, NEG)
                m_t[h, :, cols] = jnp.maximum(m_t[h, :, cols], jnp.maximum(top, second))
            return 0

        lax.fori_loop(0, nh, tile_scores, 0)
        ktt[:, span] = ktile[span, :].T
        vtt[:, span] = vtile[span, :].T

    def tile_fwd(h, _):
        for i in range(nb):
            cols = pl.ds(i * STEP, STEP)
            top = m_t[h, :, cols]
            total = jnp.zeros((1, STEP), F32)
            part = jnp.zeros((DH, STEP), F32)
            for l in range(levels):
                span = pl.ds(l * TILE, TILE)
                shift = jnp.where(valid[l], top, FAR)
                e = jnp.exp2((s_tile[h, span, cols] - shift) * factor)
                total = total + jnp.sum(e, axis=0, keepdims=True)
                e_tile[h, span, cols] = e.astype(BF16)
            part = mm(vtt[hs(h), :], e_tile[h, :, cols])
            mo = m_o[h, :, cols]
            m = jnp.maximum(mo, top)
            fo = jnp.exp2((mo - m) * factor)
            ft = jnp.exp2((top - m) * factor)
            inv = 1.0 / (fo * l_o[h, :, cols] + ft * total)
            fo = fo * inv
            ft = ft * inv
            r_o[h, :, cols] = fo
            r_t[h, :, cols] = ft
            at = acc[hs(h), cols] * fo + part * ft
            attn_t32[hs(h), cols] = at
            attn_t[hs(h), cols] = at.astype(BF16)
            attn[cols, hs(h)] = at.T.astype(BF16)
        return 0

    lax.fori_loop(0, nh, tile_fwd, 0)

    gh = width // 2
    gy = gh // ny
    gz = heads_x * width // nz
    at_rows = pl.ds(pl.multiple_of(core * gh + yy * gy, gy), gy)
    copies = {}

    def wcols(at):
        return pl.ds(pl.multiple_of(at * width, width), width)

    def yrows(at):
        return pl.ds(pl.multiple_of(at * gy, gy), gy)

    def zcols(at):
        return pl.ds(pl.multiple_of(at * gz, gz), gz)

    def half_rows(at):
        return pl.ds(pl.multiple_of(at * gh, gh), gh)

    def keep(name, *made):
        copies[name] = list(made)
        sent.extend(made)

    def arrived(name):
        for c in copies[name]:
            c.wait_recv()

    def out_over():
        p_send[0] = mm(attn[...], w_ref[:, wcols(over)]).astype(BF16)
        keep("o_lo", remote(p_send.at[0, lo], p_from.at[0, lo], x_s, x_r, 6, (b, right)))
        keep("o_hi", remote(p_send.at[0, hi], p_from.at[1, hi], x_s, x_r, 7, (b, left)))

    def out_next():
        p_send[1] = mm(attn[...], w_ref[:, wcols(right)]).astype(BF16)
        c = remote(p_send.at[1, hi], p_from.at[2, hi], x_s, x_r, 8, (b, right))
        p_send[2] = mm(attn[...], w_ref[:, wcols(left)]).astype(BF16)
        keep("near", c, remote(p_send.at[2, lo], p_from.at[3, lo], x_s, x_r, 9, (b, left)))

    def out_own():
        p_own[...] = mm(attn[...], w_ref[:, wcols(x)])

    def out_pass():
        arrived("o_lo")
        p_send[1, lo, :] = (p_send[1, lo, :].astype(F32) + p_from[0, lo, :].astype(F32)).astype(BF16)
        c = remote(p_send.at[1, lo], p_from.at[2, lo], x_s, x_r, 10, (b, right))
        arrived("o_hi")
        p_send[2, hi, :] = (p_send[2, hi, :].astype(F32) + p_from[1, hi, :].astype(F32)).astype(BF16)
        keep("passed", c, remote(p_send.at[2, hi], p_from.at[3, hi], x_s, x_r, 11, (b, left)))

    def out_end():
        arrived("near")
        arrived("passed")
        out_ref[...] = (p_own[...] + p_from[2].astype(F32) + p_from[3].astype(F32)).astype(BF16)

    def cot_all():
        to_right_hi.wait_recv()
        to_left_lo.wait_recv()
        pass_lo.wait_recv()
        pass_hi.wait_recv()

    def wg_other():
        for j in range(heads_x):
            g_send[:, pl.ds(j * width, width)] = mm(attn_t[half_rows(1 - core), :], cot[j]).astype(BF16)
        keep("core", remote(g_send, g_from, w_s, w_r, 0, sibling))

    def wg_mine():
        for j in range(heads_x):
            g_part[:, pl.ds(j * width, width)] = mm(attn_t[half_rows(core), :], cot[j])

    def wg_y():
        arrived("core")
        g_part[...] = g_part[...] + g_from[...].astype(F32)
        g_ysend[...] = g_part[...].astype(BF16)
        keep("ysum", *[
            remote(g_ysend.at[yrows(ypeer(d))], g_yfrom.at[d], w_s, w_r, d, yid(d)) for d in range(1, ny)
        ])

    def wg_z():
        arrived("ysum")
        total = g_part[yrows(yy), :]
        for d in range(1, ny):
            total = total + g_yfrom[d].astype(F32)
        g_y[...] = total
        g_zsend[...] = total.astype(BF16)
        keep("zsum", *[
            remote(g_zsend.at[:, zcols(zpeer(d))], g_zfrom.at[d], w_s, w_r, ny + d, zid(d))
            for d in range(1, nz)
        ])

    def wg_z_back():
        arrived("zsum")
        piece = g_y[:, zcols(zz)]
        for d in range(1, nz):
            piece = piece + g_zfrom[d].astype(F32)
        own = g_full.at[at_rows, zcols(zz)]
        g_full[at_rows, zcols(zz)] = piece.astype(BF16)
        keep("zall", *[remote(own, own, w_s, w_r, ny + nz + d, zid(d)) for d in range(1, nz)])

    def wg_y_back():
        arrived("zall")
        own = g_full.at[at_rows]
        made = [remote(own, own, w_s, w_r, ny + 2 * nz + d, yid(d)) for d in range(1, ny)]
        made.append(remote(own, own, w_s, w_r, 2 * ny + 2 * nz, sibling))
        keep("yall", *made[:-1])
        keep("last", made[-1])

    def wg_core_back():
        made = []
        for d in range(1, ny):
            copies["yall"][d - 1].wait_recv()
            rows_d = pl.ds(pl.multiple_of(core * gh + lax.rem(yy + ny - d, ny) * gy, gy), gy)
            got = g_full.at[rows_d]
            made.append(remote(got, got, w_s, w_r, 2 * ny + 2 * nz + d, sibling))
        keep("lasts", *made)

    def wg_end():
        arrived("last")
        arrived("lasts")
        wg_ref[...] = g_full[...].astype(F32)

    def dattn():
        for i in range(nb):
            cols = pl.ds(i * STEP, STEP)
            g = jnp.zeros((width, STEP), F32)
            for j in range(heads_x):
                g = g + mm_t(w_ref[:, pl.ds(j * width, width)], cot[j, cols, :])
            datt_t[:, cols] = g.astype(BF16)

    def spread_head(h, _):
        for i in range(nb):
            cols = pl.ds(i * STEP, STEP)
            g = datt_t[hs(h), cols].astype(F32)
            at = attn_t32[hs(h), cols]
            go = (g * r_o[h, :, cols]).astype(BF16)
            gt = (g * r_t[h, :, cols]).astype(BF16)
            datt_o[hs(h), cols] = go
            datt_s[hs(h), cols] = gt
            go = go.astype(F32)
            gt = gt.astype(F32)
            del_o[h, :, cols] = jnp.sum(go * at, axis=0, keepdims=True)
            del_t[h, :, cols] = jnp.sum(gt * at, axis=0, keepdims=True)
            datt_on[cols, hs(h)] = go.T.astype(BF16)
            datt_sn[cols, hs(h)] = gt.T.astype(BF16)
        return 0

    def spread():
        lax.fori_loop(0, nh, spread_head, 0)

    kbc, vbc = {}, {}

    def tile_bwd_for(pair):
        span = pl.ds(pair * TILE, 2 * TILE)

        def tile_bwd(h, _):
            for i in range(nb):
                cols = pl.ds(i * STEP, STEP)
                dp = mm(vtile[span, hs(h)], datt_s[hs(h), cols])
                d = e_tile[h, span, cols].astype(F32) * (dp - del_t[h, :, cols])
                d_tile[h, span, cols] = d.astype(BF16)
            dk = mm(d_tile[h, span, :], q_ref[:, hs(h)]) * scale
            dv = mm(e_tile[h, span, :], datt_sn[:, hs(h)])
            if pair == 0:
                one_b[0, :, hs(h)] = dk[TILE:]
                one_b[1, :, hs(h)] = dv[TILE:]
            ksend[span, hs(h)] = dk.astype(BF16)
            vsend[span, hs(h)] = dv.astype(BF16)
            return 0

        lax.fori_loop(0, nh, tile_bwd, 0)

    def back_k(l, to, dst):
        kbc[l] = remote(ksend.at[rows_of(l)], dst, bwd_s, bwd_r, 2 * l, to)
        sent.append(kbc[l])

    def back_v(l, to, dst):
        vbc[l] = remote(vsend.at[rows_of(l)], dst, bwd_s, bwd_r, 2 * l + 1, to)
        sent.append(vbc[l])

    def tile_z():
        tile_bwd_for(far - 1)
        back_k(2, behind(1), kmid_b)
        back_v(2, behind(1), vmid_b)
        back_v(far, mid_b, vfar_b)
        back_k(far, behind(far), kback.at[rows_of(far)])

    def tile_near():
        tile_bwd_for(0)
        tile_direct(0)

    def tile_one_send():
        kbc[2].wait_recv()
        vbc[2].wait_recv()
        ksend[rows_of(1), :] = (one_b[0] + kmid_b[...].astype(F32)).astype(BF16)
        vsend[rows_of(1), :] = (one_b[1] + vmid_b[...].astype(F32)).astype(BF16)
        back_k(1, behind(1), kback.at[rows_of(1)])
        back_v(1, behind(1), vback.at[rows_of(1)])

    def tile_far_pass():
        vbc[far].wait_recv()
        vbc[far] = remote(vfar_b, vback.at[rows_of(far)], bwd_s, bwd_r, 2 * levels, end_b)
        sent.append(vbc[far])

    def tile_direct(l):
        back_k(l, behind(l), kback.at[rows_of(l)])
        back_v(l, behind(l), vback.at[rows_of(l)])

    def tile_y():
        tile_bwd_for(levels - 2)
        for l in range(levels - 1, far, -1):
            tile_direct(l)

    def tile_end():
        dk = dqt[0]
        dv = dqt[1]
        for l in [0, 1, far] + list(range(far + 1, levels)):
            span = rows_of(l)
            kbc[l].wait_recv()
            vbc[l].wait_recv()
            dk = dk + kback[span, :].astype(F32)
            dv = dv + vback[span, :].astype(F32)
        dk_ref[last, :] = dk.astype(BF16)
        dv_ref[last, :] = dv.astype(BF16)

    def own_keys(h, j):
        span = pl.ds(j * STEP, STEP)
        for i in range(j, nb):
            cols = pl.ds(i * STEP, STEP)
            dp = mm(v_ref[span, hs(h)], datt_o[hs(h), cols])
            d = e_own[h, span, cols].astype(F32) * (dp - del_o[h, :, cols])
            d_own[h, span, cols] = d.astype(BF16)
        rest = pl.ds(j * STEP, rows - j * STEP)
        dk = mm(d_own[h, span, rest], q_ref[rest, hs(h)]) * scale
        dv = mm(e_own[h, span, rest], datt_on[rest, hs(h)])
        dk_ref[span, hs(h)] = dk.astype(BF16)
        dv_ref[span, hs(h)] = dv.astype(BF16)
        if j == nb - 1:
            dqt[0, :, hs(h)] = dk[STEP - TILE :]
            dqt[1, :, hs(h)] = dv[STEP - TILE :]

    def own_a():
        for h in range(nh):
            own_keys(h, 0)

    def own_b():
        for h in range(nh):
            for j in range(1, nb):
                own_keys(h, j)

    def own_q():
        for h in range(nh):
            for i in range(nb):
                cols = pl.ds(i * STEP, STEP)
                upto = pl.ds(0, (i + 1) * STEP)
                g = mm(kt[hs(h), upto], d_own[h, upto, cols])
                g = g + mm(ktt[hs(h), :], d_tile[h, :, cols])
                dq_ref[cols, hs(h)] = (g * scale).T.astype(BF16)

    for step in (
cot_all, wg_other, wg_mine, out_over, wg_y, out_next, dattn, spread, own_a, wg_z, tile_z, tile_near, wg_z_back, tile_one_send, wg_y_back, tile_far_pass, tile_y, out_pass, own_b, out_own, wg_core_back, own_q, wg_end, tile_end, out_end,
    ):
        step()

    for c in sent:
        c.wait_send()


def store(*refs):
    n = len(refs) // 2
    made = [pltpu.make_async_copy(refs[i], refs[n + i], refs[-1].at[i]) for i in range(n)]
    for c in made:
        c.start()
    for c in made:
        c.wait()


def local(plan, queries, keys, values, out_weight, cotangent):
    seq, heads_x, levels, ny, nz, _ = plan
    rows, width = queries.shape
    nh = width // DH
    far = levels * TILE
    wide = heads_x * width
    gh = width // 2
    gy = gh // ny
    gz = wide // nz
    dma = pltpu.SemaphoreType.DMA
    like = [(rows, width)] * 4
    shapes = [jax.ShapeDtypeStruct(s, BF16) for s in like] + [jax.ShapeDtypeStruct((width, wide), F32)]
    made = pl.pallas_call(
        functools.partial(kernel, plan),
        out_shape=[pltpu.VMEM(s, BF16) for s in like] + [pltpu.VMEM((width, wide), F32)],
        in_specs=[pl.BlockSpec(memory_space=pl.ANY)] * 5,
        out_specs=[pl.BlockSpec(memory_space=pltpu.VMEM)] * 5,
        scratch_shapes=[
            pltpu.VMEM((rows, width), BF16), pltpu.VMEM((rows, width), BF16),
            pltpu.VMEM((rows, width), BF16), pltpu.VMEM((width, wide), BF16),
            pltpu.VMEM((far, width), BF16), pltpu.VMEM((far, width), BF16),
            pltpu.VMEM((far, width), BF16), pltpu.VMEM((far, width), BF16),
            pltpu.VMEM((far, width), BF16), pltpu.VMEM((far, width), BF16),
            pltpu.VMEM((TILE, width), BF16), pltpu.VMEM((TILE, width), BF16),
            pltpu.VMEM((TILE, width), BF16), pltpu.VMEM((TILE, width), BF16),
            pltpu.VMEM((2, TILE, width), F32),
            pltpu.VMEM((heads_x, rows, width), BF16),
            pltpu.VMEM((width, rows), BF16), pltpu.VMEM((width, rows), BF16),
            pltpu.VMEM((width, far), BF16), pltpu.VMEM((width, far), BF16),
            pltpu.VMEM((rows, STEP), F32), pltpu.VMEM((nh, far, rows), F32),
            pltpu.VMEM((nh, rows, rows), BF16), pltpu.VMEM((nh, far, rows), BF16),
            pltpu.VMEM((nh, rows, rows), BF16), pltpu.VMEM((nh, far, rows), BF16),
            pltpu.VMEM((width, rows), F32), pltpu.VMEM((width, rows), F32),
            pltpu.VMEM((width, rows), BF16), pltpu.VMEM((rows, width), BF16),
        ]
        + [pltpu.VMEM((nh, 1, rows), F32)] * 7
        + [
            pltpu.VMEM((width, rows), BF16), pltpu.VMEM((width, rows), BF16),
            pltpu.VMEM((width, rows), BF16), pltpu.VMEM((rows, width), BF16),
            pltpu.VMEM((rows, width), BF16), pltpu.VMEM((2, TILE, width), F32),
            pltpu.VMEM((3, rows, width), BF16), pltpu.VMEM((rows, width), F32),
            pltpu.VMEM((4, rows, width), BF16),
            pltpu.VMEM((gh, wide), BF16), pltpu.VMEM((gh, wide), BF16),
            pltpu.VMEM((gh, wide), F32), pltpu.VMEM((gh, wide), BF16),
            pltpu.VMEM((ny, gy, wide), BF16), pltpu.VMEM((gy, wide), F32),
            pltpu.VMEM((gy, wide), BF16), pltpu.VMEM((nz, gy, gz), BF16),
            pltpu.VMEM((width, wide), BF16),
            dma((2 * levels + 1,)), dma((2 * levels + 1,)), dma((2 * levels + 1,)), dma((2 * levels + 1,)),
            dma((12,)), dma((12,)),
            dma((3 * ny + 2 * nz,)), dma((3 * ny + 2 * nz,)), dma((5,)),
        ],
        compiler_params=pltpu.CompilerParams(
            collective_id=0, has_side_effects=True, vmem_limit_bytes=52 * 1024 * 1024
        ),
        name="layer",
    )(queries, keys, values, out_weight, cotangent)
    return pl.pallas_call(
        store,
        out_shape=shapes,
        in_specs=[pl.BlockSpec(memory_space=pltpu.VMEM)] * 5,
        out_specs=[pl.BlockSpec(memory_space=pl.ANY)] * 5,
        scratch_shapes=[dma((5,))],
        name="store",
    )(*[pltpu.with_memory_space_constraint(a, pltpu.VMEM) for a in made])


def solution(mesh):
    seq = mesh.shape["seq"]
    heads_x = mesh.shape["head"]
    levels = seq.bit_length() - 1
    ny = 4 if seq >= 16 else 2
    ystride = seq // ny
    plan = (seq, heads_x, levels, ny, ystride // 2, ystride)
    return jax.shard_map(
        functools.partial(local, plan),
        mesh=mesh,
        in_specs=(
            P("seq", "head"), P("seq", "head"), P("seq", "head"), P("head", None), P("seq", "head"),
        ),
        out_specs=(
            P("seq", "head"), P("seq", "head"), P("seq", "head"), P("seq", "head"), P("head", None),
        ),
        check_vma=False,
    )
```
